256 devices in a mesh: replica: 16 (over z, core), tile: 16 (over x, y).
Axes of the slice: x: 4, y: 4, z: 8, core: 2. Of those that a mesh axis runs over, the one named last changes fastest.
Arguments:
- public_tokens: bfloat16 [4096, 5120], P('replica', 'tile'), may hold values from -6 to 6
- public_targets: bfloat16 [4096, 4096], P(('replica', 'tile')), may hold values from -6 to 6
- private_tokens: bfloat16 [6144, 5120], P('replica', 'tile'), may hold values from -6 to 6
- private_targets: bfloat16 [6144, 4096], P(('replica', 'tile')), may hold values from -6 to 6
- token_counts: int32 [16, 3], P('replica'), may hold values from 1 to 128, 320 in all within a row
- weight: float32 [5120, 4096], P('tile', 'replica'), may hold values from -0.078125 to 0.078125
- public_moment: float32 [5120, 4096], P('tile', 'replica'), may hold values from 1 to 10
- adam_first: float32 [5120, 4096], P('tile', 'replica'), may hold values from -3 to 3
- adam_second: float32 [5120, 4096], P('tile', 'replica'), may hold values from 0.1 to 1
- noise_draw: float32 [5120, 4096], P('tile', 'replica'), may hold values from -6 to 6
Outputs:
- new_weight: float32 [5120, 4096], P('tile', 'replica')
- new_first: float32 [5120, 4096], P('tile', 'replica')
- new_second: float32 [5120, 4096], P('tile', 'replica')
- new_public: float32 [5120, 4096], P('tile', 'replica')
The draws below stay inside these ranges and needn't reach their ends.
Inputs may be any that keep to these rules, and one draw needn't show every extreme that they name: `token_counts`: each row holds the live token counts of one replica's 3 private examples; every row sums to 320 and its largest entry is 128.
All inputs are finite; a program needn't handle non-finite values.
Results may differ from the reference program's by a relative error of at most 0.0031.
Values may be sent and summed in bfloat16 or wider, within the bound.
No kernel may reach another device: no remote copies, remote signals or barrier semaphores. Data moves between devices by JAX's collectives and lax.ppermute only.
A program may use at most 64 MiB of HBM per device.

```python
import math
import jax
import jax.numpy as jnp
import numpy as np
from jax import lax

D = 5120
E = 3
L = 128
Q = 4096
PUB = 4096
EXAMPLES = 48
PRIV = 6144
COUNT_SUM = 320
N_REPLICA = 16


def strengthened(entries, own_key, source, target, blocks, factor):
    owner, partner = [(jnp.arange(entries.shape[dim]) // (entries.shape[dim] // blocks)).reshape([-1 if axis == dim else 1 for axis in range(entries.ndim)]) for dim in (source, target)]
    chosen = jax.random.permutation(own_key, blocks)[partner]
    strong = (owner == chosen) | (owner == (partner + blocks // 2) % blocks)
    return jnp.where(strong, factor * entries, entries)


def shard_levels(key, extent, shards, smallest, largest):
    def one(dim, shards_of):
        heights = jax.random.uniform(jax.random.fold_in(jax.random.fold_in(key, 6), dim), (shards_of,), jnp.float32, smallest / len(shards), largest / len(shards))
        return jnp.repeat(jnp.exp(heights), extent[dim] // shards_of).reshape((-1,) + (1,) * (len(extent) - dim - 1))

    gain = one(*shards[0])
    for cut in shards[1:]:
        gain = gain * one(*cut)
    return gain


def split_up(number_of, total, most, skew):
    loads = [(1 << 20) // math.isqrt(standing ** skew) + 1 for standing in range(2, number_of + 1)]
    spare, given = total - most - (number_of - 1), [1] * (number_of - 1)
    while spare > 0:
        movable = [i for i in range(number_of - 1) if given[i] < most]
        pool, left = sum([loads[i] for i in movable]), spare
        for i in movable:
            more = min(most - given[i], max(1, left * loads[i] // pool), spare)
            given[i] = given[i] + more
            spare = spare - more
    return np.array([most] + given)


def uneven_parts(rng, count, total, bound, lean):
    if count == 2:
        one = jax.random.randint(rng, (), max(1, total - bound), min(bound, total - 1) + 1)
        return jnp.stack([one, total - one])
    tallies = jnp.asarray(split_up(count, total, bound, lean), jnp.int32)
    twos = (count - 1) // 2
    donor, taker = tallies[1:1 + 2 * twos:2], tallies[2:2 + 2 * twos:2]
    slack = jnp.minimum(donor - 1, bound - taker)
    moved = jax.random.randint(jax.random.fold_in(rng, 1), (twos,), 0, 1 << 20) % (slack + 1)
    tallies = tallies.at[1:1 + 2 * twos:2].set(donor - moved).at[2:2 + 2 * twos:2].set(taker + moved)
    return tallies[jax.random.permutation(jax.random.fold_in(rng, 2), count)]


def centred(key, shape, spread, limit, cuts=(), kind=jnp.bfloat16):
    level = shard_levels(key, shape, cuts, -0.22, 0.18) if cuts else 1.0
    array = jax.random.normal(key, shape, jnp.float32) * spread * level
    return jnp.minimum(jnp.maximum(array, -limit), limit).astype(kind)


def bell_draw_with(own_key, dims, width, most, split, heavy, held_as=jnp.bfloat16):
    entries = width * jax.random.normal(own_key, dims, jnp.float32)
    if split:
        entries = entries * shard_levels(own_key, dims, split, -0.22, 0.18)
    return jnp.clip(strengthened(entries, jax.random.fold_in(own_key, 3), *heavy), -most, most).astype(held_as)


def setup_inputs(seed: int = 0) -> dict:
    arg_keys = jax.random.split(jax.random.key(seed), 11)
    return {
        "public_tokens": bell_draw_with(arg_keys[0], (PUB, D), 1.0, 6.0, ((0, 16), (1, 16)), (1, 0, 16, 2.0)),
        "public_targets": centred(arg_keys[1], (PUB, Q), 1.0, 6.0, ((0, 256),)),
        "private_tokens": bell_draw_with(arg_keys[2], (PRIV, D), 1.0, 6.0, ((0, 16), (1, 16)), (1, 0, 16, 2.0)),
        "private_targets": centred(arg_keys[3], (PRIV, Q), 1.0, 6.0, ((0, 256),)),
        "token_counts": jax.vmap(lambda own: uneven_parts(own, E, COUNT_SUM, L, 1))(jax.random.split(arg_keys[4], N_REPLICA)).reshape((N_REPLICA, E)).astype(jnp.int32),
        "weight": centred(arg_keys[5], (D, Q), D ** -0.5, 0.078125, ((0, 16), (1, 16)), jnp.float32),
        "public_moment": jnp.clip(jnp.exp(math.log(10.0) - 2.3025851 * jax.random.uniform(arg_keys[6], (D, Q), jnp.float32) ** shard_levels(arg_keys[6], (D, Q), ((0, 16), (1, 16)), -0.2, 0.2)), 1.0, 10.0),
        "adam_first": centred(arg_keys[7], (D, Q), 0.5, 3.0, ((0, 16), (1, 16)), jnp.float32),
        "adam_second": jnp.clip(jnp.exp(math.log(1.0) - 2.3025851 * jax.random.uniform(arg_keys[8], (D, Q), jnp.float32) ** shard_levels(arg_keys[8], (D, Q), ((0, 16), (1, 16)), -0.2, 0.2)), 0.1, 1.0),
        "noise_draw": centred(arg_keys[9], (D, Q), 1.0, 6.0, ((0, 16), (1, 16)), jnp.float32),
    }


beta_first = 0.9
beta_second = 0.99
beta_public = 0.9
public_epsilon = 0.001
adam_epsilon = 1e-08
clip_factor = 0.6
noise_level = 4.0
learn_rate = 0.01

def reference(public_tokens, public_targets, private_tokens, private_targets, token_counts, weight, public_moment, adam_first, adam_second, noise_draw):
    contract = (((0,), (0,)), ((), ()))
    w_half = weight.astype(jnp.bfloat16)
    public_out = jnp.dot(public_tokens, w_half, preferred_element_type=jnp.float32)
    public_delta = (public_out - public_targets.astype(jnp.float32)).astype(jnp.bfloat16)
    public_grad = lax.dot_general(public_tokens, public_delta, contract, preferred_element_type=jnp.float32) / math.sqrt(PUB)
    new_public = beta_public * public_moment + (1.0 - beta_public) * public_grad * public_grad
    precond = 1.0 / (jnp.sqrt(new_public) + public_epsilon)
    private_out = jnp.dot(private_tokens, w_half, preferred_element_type=jnp.float32)
    row_index = jnp.arange(PRIV, dtype=jnp.int32)
    owners = (row_index // L).astype(jnp.int32)
    limits = token_counts.reshape(-1)[owners]
    valid = row_index % L < limits
    private_delta = jnp.where(valid[:, None], private_out - private_targets.astype(jnp.float32), 0.0).astype(jnp.bfloat16)

    def example_norm(example):
        first_row = (example * L).astype(jnp.int32)
        block_x = lax.dynamic_slice_in_dim(private_tokens, first_row, L, 0)
        block_d = lax.dynamic_slice_in_dim(private_delta, first_row, L, 0)
        grads = lax.dot_general(block_x, block_d, contract, preferred_element_type=jnp.float32)
        scaled = grads * precond
        return jnp.sum(scaled * scaled)
    squares = lax.map(example_norm, jnp.arange(EXAMPLES, dtype=jnp.int32))
    clip_norm = clip_factor * math.sqrt(L * D * Q)
    factors = clip_norm / jnp.maximum(jnp.sqrt(squares), clip_norm)
    weighted = (factors[owners][:, None] * private_delta.astype(jnp.float32)).astype(jnp.bfloat16)
    summed = precond * lax.dot_general(private_tokens, weighted, contract, preferred_element_type=jnp.float32)
    noise_scale = noise_level * clip_factor * math.sqrt(L)
    gradient = (summed + noise_scale * noise_draw) / EXAMPLES
    new_first = beta_first * adam_first + (1.0 - beta_first) * gradient
    new_second = beta_second * adam_second + (1.0 - beta_second) * gradient * gradient
    first_hat = new_first / (1.0 - beta_first ** 2)
    second_hat = new_second / (1.0 - beta_second ** 2)
    new_weight = weight - learn_rate * first_hat / (jnp.sqrt(second_hat) + adam_epsilon)
    return (new_weight, new_first, new_second, new_public)
```

```python
import math

import jax
import jax.numpy as jnp
from jax import lax
from jax.sharding import PartitionSpec as P

D = 5120
L = 128
Q = 4096


beta_first = 0.9
beta_second = 0.99
beta_public = 0.9
public_epsilon = 0.001
adam_epsilon = 1e-08
clip_factor = 0.6
noise_level = 4.0
learn_rate = 0.01


def regroup(rows, tiles):
    groups, span, cols = rows.shape
    split = rows.reshape(groups, tiles, span // tiles, cols)
    return split.transpose(1, 0, 2, 3).reshape(tiles, groups * (span // tiles), cols)


def ungroup(rows, groups):
    tiles, span, cols = rows.shape
    split = rows.reshape(tiles, groups, span // groups, cols)
    return split.transpose(1, 0, 2, 3).reshape(groups, tiles * (span // groups), cols)


def sum_everywhere(values, axis):
    parts = lax.axis_size(axis)
    sent = jnp.broadcast_to(values[None], (parts, *values.shape))
    return jnp.sum(lax.all_to_all(sent, axis, 0, 0, tiled=True), axis=0)


def on_device(
    public_tokens,
    public_targets,
    private_tokens,
    private_targets,
    token_counts,
    weight,
    public_moment,
    adam_first,
    adam_second,
    noise_draw,
):
    replicas = lax.axis_size("replica")
    tiles = lax.axis_size("tile")
    pub = public_tokens.shape[0]
    priv = private_tokens.shape[0]
    cols = weight.shape[1]
    examples_here = token_counts.shape[1]

    live = (
        jnp.arange(L, dtype=jnp.int32)[None, :] < token_counts[0][:, None]
    ).reshape(priv)
    live_tokens = jnp.where(live[:, None], private_tokens, jnp.zeros_like(private_tokens))
    local = jnp.concatenate([public_tokens.T, live_tokens.T], axis=1)
    tokens = lax.all_gather(local, "replica", axis=0)

    targets = jnp.concatenate([public_targets, private_targets], axis=0)
    targets = targets.reshape(-1, replicas, cols).transpose(1, 0, 2)
    targets = lax.all_to_all(targets, "replica", 0, 0, tiled=True)
    pub_rows = public_targets.shape[0]
    targets = jnp.concatenate(
        [
            targets[:, :pub_rows].reshape(pub, cols),
            targets[:, pub_rows:].reshape(priv, cols),
        ],
        axis=0,
    )

    out = jnp.einsum(
        "rfn,fc->rnc",
        tokens,
        weight.astype(jnp.bfloat16),
        preferred_element_type=jnp.float32,
    ).astype(jnp.bfloat16)
    sent = jnp.concatenate(
        [regroup(out[:, :pub], tiles), regroup(out[:, pub:], tiles)], axis=1
    )
    got = lax.all_to_all(sent, "tile", 0, 0, tiled=True)
    total = jnp.sum(got.astype(jnp.float32), axis=0)
    delta = (total - targets.astype(jnp.float32)).astype(jnp.bfloat16)
    deltas = lax.all_gather(delta, "tile", axis=0)
    public_delta = ungroup(deltas[:, :pub], replicas)
    private_delta = ungroup(deltas[:, pub:], replicas)

    public_grad = jnp.einsum(
        "rfn,rnc->fc", tokens[:, :, :pub], public_delta, preferred_element_type=jnp.float32
    ) / math.sqrt(pub * replicas)
    new_public = beta_public * public_moment + (1.0 - beta_public) * public_grad * public_grad
    precond = 1.0 / (jnp.sqrt(new_public) + public_epsilon)

    grads = jnp.einsum(
        "rfek,rekc->refc",
        tokens[:, :, pub:].reshape(replicas, -1, examples_here, L),
        private_delta.reshape(replicas, examples_here, L, cols),
        preferred_element_type=jnp.float32,
    )
    scaled = grads * precond
    squares = jnp.sum(scaled * scaled, axis=(2, 3))
    squares = sum_everywhere(sum_everywhere(squares, "tile"), "replica")
    clip_norm = clip_factor * math.sqrt(L * D * Q)
    factors = clip_norm / jnp.maximum(jnp.sqrt(squares), clip_norm)
    summed = precond * jnp.sum(factors[:, :, None, None] * grads, axis=(0, 1))

    examples_total = examples_here * replicas
    noise_scale = noise_level * clip_factor * math.sqrt(L)
    gradient = (summed + noise_scale * noise_draw) / examples_total
    new_first = beta_first * adam_first + (1.0 - beta_first) * gradient
    new_second = beta_second * adam_second + (1.0 - beta_second) * gradient * gradient
    first_hat = new_first / (1.0 - beta_first**2)
    second_hat = new_second / (1.0 - beta_second**2)
    new_weight = weight - learn_rate * first_hat / (jnp.sqrt(second_hat) + adam_epsilon)
    return (new_weight, new_first, new_second, new_public)


def solution(mesh):
    placed = (
        P("replica", "tile"),
        P(("replica", "tile"), None),
        P("replica", "tile"),
        P(("replica", "tile"), None),
        P("replica", None),
        P("tile", "replica"),
        P("tile", "replica"),
        P("tile", "replica"),
        P("tile", "replica"),
        P("tile", "replica"),
    )
    return jax.shard_map(
        on_device,
        mesh=mesh,
        in_specs=placed,
        out_specs=(
            P("tile", "replica"),
            P("tile", "replica"),
            P("tile", "replica"),
            P("tile", "replica"),
        ),
        check_vma=False,
    )
```

```python
import math

import jax
import jax.numpy as jnp
from jax import lax
from jax.sharding import PartitionSpec as P

D = 5120
L = 128
Q = 4096
CORES = 2


beta_first = 0.9
beta_second = 0.99
beta_public = 0.9
public_epsilon = 0.001
adam_epsilon = 1e-08
clip_factor = 0.6
noise_level = 4.0
learn_rate = 0.01


def regroup(rows, tiles):
    groups, span, cols = rows.shape
    split = rows.reshape(groups, tiles, span // tiles, cols)
    return split.transpose(1, 0, 2, 3).reshape(tiles, groups * (span // tiles), cols)


def ungroup(rows, groups):
    tiles, span, cols = rows.shape
    split = rows.reshape(tiles, groups, span // groups, cols)
    return split.transpose(1, 0, 2, 3).reshape(groups, tiles * (span // groups), cols)


def exchange(sent, axis, groups, kept=()):
    sent, kept = lax.optimization_barrier((sent, kept))
    got = lax.all_to_all(sent, axis, 0, 0, tiled=True, axis_index_groups=groups)
    return lax.optimization_barrier((got, kept))


def everywhere(values, parts):
    return jnp.broadcast_to(values[None], (parts, *values.shape))


def on_device(
    public_tokens,
    public_targets,
    private_tokens,
    private_targets,
    token_counts,
    weight,
    public_moment,
    adam_first,
    adam_second,
    noise_draw,
):
    replicas = lax.axis_size("replica")
    tiles = lax.axis_size("tile")
    chips = replicas // CORES
    core = lax.axis_index("replica") % CORES
    stacks = [[CORES * z + c for z in range(chips)] for c in range(CORES)]
    pub = public_tokens.shape[0]
    priv = private_tokens.shape[0]
    rows = weight.shape[0]
    cols = weight.shape[1]
    wide = CORES * cols
    examples_here = token_counts.shape[1]
    pub_rows = public_targets.shape[0]
    priv_rows = private_targets.shape[0]

    def partner(values):
        swap = [(r, r ^ 1) for r in range(replicas)]
        return lax.ppermute(values, "replica", swap)

    live = (
        jnp.arange(L, dtype=jnp.int32)[None, :] < token_counts[0][:, None]
    ).reshape(priv)
    live_tokens = jnp.where(live[:, None], private_tokens, jnp.zeros_like(private_tokens))
    local = jnp.concatenate([public_tokens.T, live_tokens.T], axis=1)
    tokens = lax.all_gather(local, "replica", axis=0, axis_index_groups=stacks)

    w_half = weight.astype(jnp.bfloat16)
    w_wide = jnp.concatenate([w_half, partner(w_half)], axis=1)

    targets = jnp.concatenate([public_targets, private_targets], axis=0)
    targets = targets.reshape(-1, chips, CORES, cols)
    targets = jnp.where(core == 0, targets, targets[:, :, ::-1])
    targets = targets.reshape(-1, chips, wide).transpose(1, 0, 2)
    targets = lax.all_to_all(
        targets, "replica", 0, 0, tiled=True, axis_index_groups=stacks
    )
    targets = jnp.concatenate(
        [
            targets[:, :pub_rows].reshape(chips * pub_rows, wide),
            targets[:, pub_rows:].reshape(chips * priv_rows, wide),
        ],
        axis=0,
    )

    out = jnp.einsum(
        "zfn,fk->znk", tokens, w_wide, preferred_element_type=jnp.float32
    ).astype(jnp.bfloat16)
    sent = jnp.concatenate(
        [regroup(out[:, :pub], tiles), regroup(out[:, pub:], tiles)], axis=1
    )
    got, (targets, tokens) = exchange(sent, "tile", None, (targets, tokens))
    total = jnp.sum(got.astype(jnp.float32), axis=0)
    delta = (total - targets.astype(jnp.float32)).astype(jnp.bfloat16)
    deltas, (tokens, public_moment) = exchange(
        everywhere(delta, tiles), "tile", None, (tokens, public_moment)
    )
    pub_all = chips * pub_rows
    public_delta = ungroup(deltas[:, :pub_all], chips)
    private_delta = ungroup(deltas[:, pub_all:], chips)

    public_grad = jnp.einsum(
        "zfn,znk->fk", tokens[:, :, :pub], public_delta, preferred_element_type=jnp.float32
    )
    public_grad = (public_grad[:, :cols] + partner(public_grad[:, cols:])) / math.sqrt(
        pub * replicas
    )
    new_public = beta_public * public_moment + (1.0 - beta_public) * public_grad * public_grad
    precond = 1.0 / (jnp.sqrt(new_public) + public_epsilon)
    precond_wide = jnp.concatenate([precond, partner(precond)], axis=1)

    grads = jnp.einsum(
        "zfel,zelk->zefk",
        tokens[:, :, pub:].reshape(chips, rows, examples_here, L),
        private_delta.reshape(chips, examples_here, L, wide),
        preferred_element_type=jnp.float32,
    )
    scaled = grads * precond_wide
    squares = jnp.sum(scaled * scaled, axis=(2, 3))
    squares = jnp.sum(exchange(everywhere(squares, tiles), "tile", None)[0], axis=0)
    squares = jnp.sum(exchange(everywhere(squares, chips), "replica", stacks)[0], axis=0)
    clip_norm = clip_factor * math.sqrt(L * D * Q)
    factors = clip_norm / jnp.maximum(jnp.sqrt(squares), clip_norm)
    summed = jnp.sum(factors[:, :, None, None] * grads, axis=(0, 1))
    summed = precond * (summed[:, :cols] + partner(summed[:, cols:]))

    examples_total = examples_here * replicas
    noise_scale = noise_level * clip_factor * math.sqrt(L)
    gradient = (summed + noise_scale * noise_draw) / examples_total
    new_first = beta_first * adam_first + (1.0 - beta_first) * gradient
    new_second = beta_second * adam_second + (1.0 - beta_second) * gradient * gradient
    first_hat = new_first / (1.0 - beta_first**2)
    second_hat = new_second / (1.0 - beta_second**2)
    new_weight = weight - learn_rate * first_hat / (jnp.sqrt(second_hat) + adam_epsilon)
    return (new_weight, new_first, new_second, new_public)


def solution(mesh):
    placed = (
        P("replica", "tile"),
        P(("replica", "tile"), None),
        P("replica", "tile"),
        P(("replica", "tile"), None),
        P("replica", None),
        P("tile", "replica"),
        P("tile", "replica"),
        P("tile", "replica"),
        P("tile", "replica"),
        P("tile", "replica"),
    )
    return jax.shard_map(
        on_device,
        mesh=mesh,
        in_specs=placed,
        out_specs=(
            P("tile", "replica"),
            P("tile", "replica"),
            P("tile", "replica"),
            P("tile", "replica"),
        ),
        check_vma=False,
    )
```

```python
import math

import jax
import jax.numpy as jnp
from jax import lax
from jax.sharding import PartitionSpec as P

D = 5120
L = 128
Q = 4096
CORES = 2
SIDE = 4


beta_first = 0.9
beta_second = 0.99
beta_public = 0.9
public_epsilon = 0.001
adam_epsilon = 1e-08
clip_factor = 0.6
noise_level = 4.0
learn_rate = 0.01


def exchange(sent, axis, groups, kept=()):
    sent, kept = lax.optimization_barrier((sent, kept))
    got = lax.all_to_all(sent, axis, 0, 0, tiled=True, axis_index_groups=groups)
    return lax.optimization_barrier((got, kept))


def everywhere(values, parts):
    return jnp.broadcast_to(values[None], (parts, *values.shape))


def to_class(replicas):
    tiles = SIDE * SIDE
    moves = []
    for replica in range(replicas):
        quad, inner = divmod(replica, CORES * 2)
        odd, core = divmod(inner, CORES)
        for tile in range(tiles):
            x, y = divmod(tile, SIDE)
            target = (quad * SIDE + x) * tiles + (odd + 2 * core) * SIDE + y
            moves.append((replica * tiles + tile, target))
    return moves


def on_device(
    public_tokens,
    public_targets,
    private_tokens,
    private_targets,
    token_counts,
    weight,
    public_moment,
    adam_first,
    adam_second,
    noise_draw,
):
    replicas = lax.axis_size("replica")
    along_x = [[x * SIDE + y for x in range(SIDE)] for y in range(SIDE)]
    along_y = [[x * SIDE + y for y in range(SIDE)] for x in range(SIDE)]
    quads = replicas // SIDE
    pub = public_tokens.shape[0]
    priv = private_tokens.shape[0]
    rows, cols = weight.shape
    examples_here = token_counts.shape[1]
    pub_rows = public_targets.shape[0]
    priv_rows = private_targets.shape[0]
    pub_all = quads * SIDE * pub_rows
    priv_all = quads * SIDE * priv_rows
    moves = to_class(replicas)

    live = (
        jnp.arange(L, dtype=jnp.int32)[None, :] < token_counts[0][:, None]
    ).reshape(priv)
    live_tokens = jnp.where(live[:, None], private_tokens, jnp.zeros_like(private_tokens))
    local = jnp.concatenate([public_tokens.T, live_tokens.T], axis=1)
    local = lax.ppermute(local, ("replica", "tile"), moves)
    tokens = lax.all_gather(local, "replica", axis=0)
    tokens = tokens.reshape(quads, SIDE, rows, pub + priv)

    w_half = weight.astype(jnp.bfloat16)
    w_group = lax.all_to_all(
        everywhere(w_half, SIDE), "tile", 0, 0, tiled=True, axis_index_groups=along_x
    )

    targets = jnp.concatenate([public_targets, private_targets], axis=0)
    targets = lax.ppermute(targets, ("replica", "tile"), moves)
    targets = targets.reshape(-1, replicas, cols).transpose(1, 0, 2)
    targets = lax.all_to_all(targets, "replica", 0, 0, tiled=True)
    targets = jnp.concatenate(
        [
            targets[:, :pub_rows].reshape(pub_all, cols),
            targets[:, pub_rows:].reshape(priv_all, cols),
        ],
        axis=0,
    )

    def by_owner(part, span):
        part = part.reshape(quads, SIDE, SIDE, span, cols)
        return part.transpose(2, 0, 1, 3, 4).reshape(SIDE, quads * SIDE * span, cols)

    def by_token(part, span):
        part = part.reshape(SIDE, quads, SIDE, span, cols)
        return part.transpose(1, 2, 0, 3, 4).reshape(quads, SIDE * SIDE * span, cols)

    out = jnp.einsum(
        "qxfn,xfk->qnk", tokens, w_group, preferred_element_type=jnp.float32
    ).astype(jnp.bfloat16)
    sent = jnp.concatenate(
        [by_owner(out[:, :pub], pub_rows), by_owner(out[:, pub:], priv_rows)], axis=1
    )
    got, (targets, tokens) = exchange(sent, "tile", along_y, (targets, tokens))
    total = jnp.sum(got.astype(jnp.float32), axis=0)
    delta = (total - targets.astype(jnp.float32)).astype(jnp.bfloat16)
    deltas, (tokens, public_moment) = exchange(
        everywhere(delta, SIDE), "tile", along_y, (tokens, public_moment)
    )
    public_delta = by_token(deltas[:, :pub_all], pub_rows)
    private_delta = by_token(deltas[:, pub_all:], priv_rows)

    def over_classes(part):
        got, _ = exchange(part.astype(jnp.bfloat16), "tile", along_x)
        return jnp.sum(got.astype(jnp.float32), axis=0)

    public_grad = over_classes(
        jnp.einsum(
            "qxfn,qnk->xfk",
            tokens[:, :, :, :pub],
            public_delta,
            preferred_element_type=jnp.float32,
        )
    ) / math.sqrt(pub * replicas)
    new_public = beta_public * public_moment + (1.0 - beta_public) * public_grad * public_grad
    precond = 1.0 / (jnp.sqrt(new_public) + public_epsilon)
    precond_group, _ = exchange(
        everywhere(precond.astype(jnp.bfloat16), SIDE), "tile", along_x
    )

    grads = jnp.einsum(
        "qxfel,qelk->qexfk",
        tokens[:, :, :, pub:].reshape(quads, SIDE, rows, examples_here, L),
        private_delta.reshape(quads, examples_here, L, cols),
        preferred_element_type=jnp.float32,
    )
    scaled = grads * precond_group.astype(jnp.float32)
    squares = jnp.sum(scaled * scaled, axis=(2, 3, 4))
    squares = jnp.sum(exchange(everywhere(squares, SIDE), "tile", along_y)[0], axis=0)
    squares = jnp.sum(exchange(everywhere(squares, replicas), "replica", None)[0], axis=0)
    clip_norm = clip_factor * math.sqrt(L * D * Q)
    factors = clip_norm / jnp.maximum(jnp.sqrt(squares), clip_norm)
    summed = jnp.sum(factors[:, :, None, None, None] * grads, axis=(0, 1))
    summed = precond * over_classes(summed)

    examples_total = examples_here * replicas
    noise_scale = noise_level * clip_factor * math.sqrt(L)
    gradient = (summed + noise_scale * noise_draw) / examples_total
    new_first = beta_first * adam_first + (1.0 - beta_first) * gradient
    new_second = beta_second * adam_second + (1.0 - beta_second) * gradient * gradient
    first_hat = new_first / (1.0 - beta_first**2)
    second_hat = new_second / (1.0 - beta_second**2)
    new_weight = weight - learn_rate * first_hat / (jnp.sqrt(second_hat) + adam_epsilon)
    return (new_weight, new_first, new_second, new_public)


def solution(mesh):
    placed = (
        P("replica", "tile"),
        P(("replica", "tile"), None),
        P("replica", "tile"),
        P(("replica", "tile"), None),
        P("replica", None),
        P("tile", "replica"),
        P("tile", "replica"),
        P("tile", "replica"),
        P("tile", "replica"),
        P("tile", "replica"),
    )
    return jax.shard_map(
        on_device,
        mesh=mesh,
        in_specs=placed,
        out_specs=(
            P("tile", "replica"),
            P("tile", "replica"),
            P("tile", "replica"),
            P("tile", "replica"),
        ),
        check_vma=False,
    )
```

```python
import math

import jax
import jax.numpy as jnp
from jax import lax
from jax.experimental import pallas as pl
from jax.experimental.pallas import tpu as pltpu
from jax.sharding import PartitionSpec as P

D = 5120
L = 128
Q = 4096
CORES = 2
SIDE = 4


beta_first = 0.9
beta_second = 0.99
beta_public = 0.9
public_epsilon = 0.001
adam_epsilon = 1e-08
clip_factor = 0.6
noise_level = 4.0
learn_rate = 0.01


def exchange(sent, axis, groups, kept=()):
    sent, kept = lax.optimization_barrier((sent, kept))
    got = lax.all_to_all(sent, axis, 0, 0, tiled=True, axis_index_groups=groups)
    return lax.optimization_barrier((got, kept))


def everywhere(values, parts):
    return jnp.broadcast_to(values[None], (parts, *values.shape))


def to_class(replicas):
    tiles = SIDE * SIDE
    moves = []
    for replica in range(replicas):
        quad, inner = divmod(replica, CORES * 2)
        odd, core = divmod(inner, CORES)
        for tile in range(tiles):
            x, y = divmod(tile, SIDE)
            target = (quad * SIDE + x) * tiles + (odd + 2 * core) * SIDE + y
            moves.append((replica * tiles + tile, target))
    return moves


def norms_kernel(pub, tokens_ref, delta_ref, precond_ref, out_ref):
    sides, rows = tokens_ref.shape[1], tokens_ref.shape[2]
    examples = delta_ref.shape[1] // L
    row_at = lax.broadcasted_iota(jnp.int32, out_ref.shape[1:], 0)
    found = jnp.zeros(out_ref.shape[1:], jnp.float32)
    for example in range(examples):
        block_d = delta_ref[0, example * L : (example + 1) * L, :]
        first = pub + example * L
        acc = jnp.zeros((8, block_d.shape[1]), jnp.float32)
        for side in range(sides):
            grads = jnp.dot(
                tokens_ref[0, side, :, first : first + L],
                block_d,
                preferred_element_type=jnp.float32,
            )
            scaled = grads * precond_ref[side].astype(jnp.float32)
            acc = acc + jnp.sum((scaled * scaled).reshape(rows // 8, 8, -1), axis=0)
        found = jnp.where(row_at == example, jnp.sum(acc), found)
    out_ref[0] = found


def example_squares(tokens, deltas, precond, pub):
    quads, sides, rows, span = tokens.shape
    priv, cols = deltas.shape[1:]
    out = pl.pallas_call(
        lambda *refs: norms_kernel(pub, *refs),
        grid=(quads,),
        in_specs=[
            pl.BlockSpec((1, sides, rows, span), lambda q: (q, 0, 0, 0)),
            pl.BlockSpec((1, priv, cols), lambda q: (q, 0, 0)),
            pl.BlockSpec((sides, rows, cols), lambda q: (0, 0, 0)),
        ],
        out_specs=pl.BlockSpec((1, 8, L), lambda q: (q, 0, 0)),
        out_shape=jax.ShapeDtypeStruct((quads, 8, L), jnp.float32),
        name="example_squares",
    )(tokens, deltas, precond)
    return out[:, : priv // L, 0]


def clipped_kernel(pub, factors_ref, tokens_ref, delta_ref, out_ref, acc_ref):
    quad = pl.program_id(0)
    examples = delta_ref.shape[1] // L
    weighted = jnp.concatenate(
        [
            (
                factors_ref[quad, example]
                * delta_ref[0, example * L : (example + 1) * L, :].astype(jnp.float32)
            ).astype(jnp.bfloat16)
            for example in range(examples)
        ],
        axis=0,
    )

    @pl.when(quad == 0)
    def _():
        acc_ref[...] = jnp.zeros_like(acc_ref)

    for side in range(tokens_ref.shape[1]):
        acc_ref[side] += jnp.dot(
            tokens_ref[0, side, :, pub:], weighted, preferred_element_type=jnp.float32
        )

    @pl.when(quad == pl.num_programs(0) - 1)
    def _():
        out_ref[...] = acc_ref[...].astype(out_ref.dtype)


def clipped_sum(factors, tokens, deltas, pub):
    quads, sides, rows, span = tokens.shape
    priv, cols = deltas.shape[1:]
    return pl.pallas_call(
        lambda *refs: clipped_kernel(pub, *refs),
        grid=(quads,),
        in_specs=[
            pl.BlockSpec(memory_space=pltpu.SMEM),
            pl.BlockSpec((1, sides, rows, span), lambda q: (q, 0, 0, 0)),
            pl.BlockSpec((1, priv, cols), lambda q: (q, 0, 0)),
        ],
        out_specs=pl.BlockSpec((sides, rows, cols), lambda q: (0, 0, 0)),
        out_shape=jax.ShapeDtypeStruct((sides, rows, cols), jnp.bfloat16),
        scratch_shapes=[pltpu.VMEM((sides, rows, cols), jnp.float32)],
        name="clipped_sum",
    )(factors, tokens, deltas)


def on_device(
    public_tokens,
    public_targets,
    private_tokens,
    private_targets,
    token_counts,
    weight,
    public_moment,
    adam_first,
    adam_second,
    noise_draw,
):
    replicas = lax.axis_size("replica")
    along_x = [[x * SIDE + y for x in range(SIDE)] for y in range(SIDE)]
    along_y = [[x * SIDE + y for y in range(SIDE)] for x in range(SIDE)]
    quads = replicas // SIDE
    pub = public_tokens.shape[0]
    priv = private_tokens.shape[0]
    rows, cols = weight.shape
    examples_here = token_counts.shape[1]
    pub_rows = public_targets.shape[0]
    priv_rows = private_targets.shape[0]
    pub_all = quads * SIDE * pub_rows
    priv_all = quads * SIDE * priv_rows
    moves = to_class(replicas)

    live = (
        jnp.arange(L, dtype=jnp.int32)[None, :] < token_counts[0][:, None]
    ).reshape(priv)
    live_tokens = jnp.where(live[:, None], private_tokens, jnp.zeros_like(private_tokens))
    local = jnp.concatenate([public_tokens.T, live_tokens.T], axis=1)
    local = lax.ppermute(local, ("replica", "tile"), moves)
    tokens = lax.all_gather(local, "replica", axis=0)
    tokens = tokens.reshape(quads, SIDE, rows, pub + priv)

    w_half = weight.astype(jnp.bfloat16)
    w_group = lax.all_to_all(
        everywhere(w_half, SIDE), "tile", 0, 0, tiled=True, axis_index_groups=along_x
    )

    targets = jnp.concatenate([public_targets, private_targets], axis=0)
    targets = lax.ppermute(targets, ("replica", "tile"), moves)
    targets = targets.reshape(-1, replicas, cols).transpose(1, 0, 2)
    targets = lax.all_to_all(targets, "replica", 0, 0, tiled=True)
    targets = jnp.concatenate(
        [
            targets[:, :pub_rows].reshape(pub_all, cols),
            targets[:, pub_rows:].reshape(priv_all, cols),
        ],
        axis=0,
    )

    def by_owner(part, span):
        part = part.reshape(quads, SIDE, SIDE, span, cols)
        return part.transpose(2, 0, 1, 3, 4).reshape(SIDE, quads * SIDE * span, cols)

    def by_token(part, span):
        part = part.reshape(SIDE, quads, SIDE, span, cols)
        return part.transpose(1, 2, 0, 3, 4).reshape(quads, SIDE * SIDE * span, cols)

    out = jnp.einsum(
        "qxfn,xfk->qnk", tokens, w_group, preferred_element_type=jnp.float32
    ).astype(jnp.bfloat16)
    sent = jnp.concatenate(
        [by_owner(out[:, :pub], pub_rows), by_owner(out[:, pub:], priv_rows)], axis=1
    )
    got, (targets, tokens) = exchange(sent, "tile", along_y, (targets, tokens))
    total = jnp.sum(got.astype(jnp.float32), axis=0)
    delta = (total - targets.astype(jnp.float32)).astype(jnp.bfloat16)
    deltas, (tokens, public_moment) = exchange(
        everywhere(delta, SIDE), "tile", along_y, (tokens, public_moment)
    )
    public_delta = by_token(deltas[:, :pub_all], pub_rows)
    private_delta = by_token(deltas[:, pub_all:], priv_rows)

    def over_classes(part):
        got, _ = exchange(part.astype(jnp.bfloat16), "tile", along_x)
        return jnp.sum(got.astype(jnp.float32), axis=0)

    public_grad = over_classes(
        jnp.einsum(
            "qxfn,qnk->xfk",
            tokens[:, :, :, :pub],
            public_delta,
            preferred_element_type=jnp.float32,
        )
    ) / math.sqrt(pub * replicas)
    new_public = beta_public * public_moment + (1.0 - beta_public) * public_grad * public_grad
    precond = 1.0 / (jnp.sqrt(new_public) + public_epsilon)
    precond_group, _ = exchange(
        everywhere(precond.astype(jnp.bfloat16), SIDE), "tile", along_x
    )

    squares = example_squares(
        tokens, private_delta, precond_group, pub
    )
    squares = jnp.sum(exchange(everywhere(squares, SIDE), "tile", along_y)[0], axis=0)
    squares = jnp.sum(exchange(everywhere(squares, replicas), "replica", None)[0], axis=0)
    clip_norm = clip_factor * math.sqrt(L * D * Q)
    factors = clip_norm / jnp.maximum(jnp.sqrt(squares), clip_norm)
    summed = precond * over_classes(clipped_sum(factors, tokens, private_delta, pub))

    examples_total = examples_here * replicas
    noise_scale = noise_level * clip_factor * math.sqrt(L)
    gradient = (summed + noise_scale * noise_draw) / examples_total
    new_first = beta_first * adam_first + (1.0 - beta_first) * gradient
    new_second = beta_second * adam_second + (1.0 - beta_second) * gradient * gradient
    first_hat = new_first / (1.0 - beta_first**2)
    second_hat = new_second / (1.0 - beta_second**2)
    new_weight = weight - learn_rate * first_hat / (jnp.sqrt(second_hat) + adam_epsilon)
    return (new_weight, new_first, new_second, new_public)


def solution(mesh):
    placed = (
        P("replica", "tile"),
        P(("replica", "tile"), None),
        P("replica", "tile"),
        P(("replica", "tile"), None),
        P("replica", None),
        P("tile", "replica"),
        P("tile", "replica"),
        P("tile", "replica"),
        P("tile", "replica"),
        P("tile", "replica"),
    )
    return jax.shard_map(
        on_device,
        mesh=mesh,
        in_specs=placed,
        out_specs=(
            P("tile", "replica"),
            P("tile", "replica"),
            P("tile", "replica"),
            P("tile", "replica"),
        ),
        check_vma=False,
    )
```

```python
import math

import jax
import jax.numpy as jnp
from jax import lax
from jax.experimental import pallas as pl
from jax.experimental.pallas import tpu as pltpu
from jax.sharding import PartitionSpec as P

D = 5120
L = 128
Q = 4096
CORES = 2
SIDE = 4


beta_first = 0.9
beta_second = 0.99
beta_public = 0.9
public_epsilon = 0.001
adam_epsilon = 1e-08
clip_factor = 0.6
noise_level = 4.0
learn_rate = 0.01


def exchange(sent, axis, groups, kept=()):
    sent, kept = lax.optimization_barrier((sent, kept))
    got = lax.all_to_all(sent, axis, 0, 0, tiled=True, axis_index_groups=groups)
    return lax.optimization_barrier((got, kept))


def everywhere(values, parts):
    return jnp.broadcast_to(values[None], (parts, *values.shape))


def to_class(replicas):
    tiles = SIDE * SIDE
    moves = []
    for replica in range(replicas):
        quad, inner = divmod(replica, CORES * 2)
        odd, core = divmod(inner, CORES)
        for tile in range(tiles):
            x, y = divmod(tile, SIDE)
            target = (quad * SIDE + x) * tiles + (odd + 2 * core) * SIDE + y
            moves.append((replica * tiles + tile, target))
    return moves


def token_sides(tokens_ref):
    return [(b, h) for b in range(tokens_ref.shape[0]) for h in range(tokens_ref.shape[2])]


def token_spec(tokens):
    cores, _, halves, rows, span = tokens.shape
    return pl.BlockSpec((cores, 1, halves, rows, span), lambda q: (0, q, 0, 0, 0))


def outputs_kernel(pub, spans, tokens_ref, w_ref, out_ref):
    span = tokens_ref.shape[4]
    total = jnp.zeros((span, w_ref.shape[2]), jnp.float32)
    for side, (b, h) in enumerate(token_sides(tokens_ref)):
        total = total + lax.dot_general(
            tokens_ref[b, 0, h],
            w_ref[side],
            (((0,), (0,)), ((), ())),
            preferred_element_type=jnp.float32,
        )
    for owner in range(SIDE):
        pieces = []
        for first, rows in ((0, spans[0]), (pub, spans[1])):
            for x in range(SIDE):
                at = first + (x * SIDE + owner) * rows
                pieces.append(total[at : at + rows])
        out_ref[owner, 0] = jnp.concatenate(pieces, axis=0).astype(out_ref.dtype)


def outputs_by_owner(tokens, w_group, pub, spans):
    quads = tokens.shape[1]
    chunk, cols = SIDE * sum(spans), w_group.shape[2]
    return pl.pallas_call(
        lambda *refs: outputs_kernel(pub, spans, *refs),
        grid=(quads,),
        in_specs=[token_spec(tokens), pl.BlockSpec(w_group.shape, lambda q: (0, 0, 0))],
        out_specs=pl.BlockSpec((SIDE, 1, chunk, cols), lambda q: (0, q, 0, 0)),
        out_shape=jax.ShapeDtypeStruct((SIDE, quads, chunk, cols), jnp.bfloat16),
        name="outputs_by_owner",
    )(tokens, w_group)


def public_kernel(pub, spans, tokens_ref, deltas_ref, out_ref, private_ref, acc_ref):
    quad = pl.program_id(0)
    deltas = deltas_ref[:, 0].astype(jnp.float32)
    ordered = []
    for first, rows in ((0, spans[0]), (SIDE * spans[0], spans[1])):
        pieces = [
            deltas[owner, first + x * rows : first + (x + 1) * rows]
            for x in range(SIDE)
            for owner in range(SIDE)
        ]
        ordered.append(jnp.concatenate(pieces, axis=0).astype(jnp.bfloat16))
    private_ref[0] = ordered[1]

    @pl.when(quad == 0)
    def _():
        acc_ref[...] = jnp.zeros_like(acc_ref)

    for side, (b, h) in enumerate(token_sides(tokens_ref)):
        acc_ref[side] += jnp.dot(
            tokens_ref[b, 0, h, :, :pub], ordered[0], preferred_element_type=jnp.float32
        )

    @pl.when(quad == pl.num_programs(0) - 1)
    def _():
        out_ref[...] = acc_ref[...].astype(out_ref.dtype)


def public_product(tokens, deltas, pub, spans):
    cores, quads, halves, rows, span = tokens.shape
    chunk, cols = deltas.shape[2:]
    whole = (cores * halves, rows, cols)
    return pl.pallas_call(
        lambda *refs: public_kernel(pub, spans, *refs),
        grid=(quads,),
        in_specs=[
            token_spec(tokens),
            pl.BlockSpec((SIDE, 1, chunk, cols), lambda q: (0, q, 0, 0)),
        ],
        out_specs=[
            pl.BlockSpec(whole, lambda q: (0, 0, 0)),
            pl.BlockSpec((1, span - pub, cols), lambda q: (q, 0, 0)),
        ],
        out_shape=[
            jax.ShapeDtypeStruct(whole, jnp.bfloat16),
            jax.ShapeDtypeStruct((quads, span - pub, cols), jnp.bfloat16),
        ],
        scratch_shapes=[pltpu.VMEM(whole, jnp.float32)],
        name="public_product",
    )(tokens, deltas)


def norms_kernel(pub, tokens_ref, delta_ref, precond_ref, out_ref):
    rows = tokens_ref.shape[3]
    examples = delta_ref.shape[1] // L
    row_at = lax.broadcasted_iota(jnp.int32, out_ref.shape[1:], 0)
    found = jnp.zeros(out_ref.shape[1:], jnp.float32)
    for example in range(examples):
        block_d = delta_ref[0, example * L : (example + 1) * L, :]
        first = pub + example * L
        acc = jnp.zeros((8, block_d.shape[1]), jnp.float32)
        for side, (b, h) in enumerate(token_sides(tokens_ref)):
            grads = jnp.dot(
                tokens_ref[b, 0, h, :, first : first + L],
                block_d,
                preferred_element_type=jnp.float32,
            )
            scaled = grads * precond_ref[side].astype(jnp.float32)
            acc = acc + jnp.sum((scaled * scaled).reshape(rows // 8, 8, -1), axis=0)
        found = jnp.where(row_at == example, jnp.sum(acc), found)
    out_ref[0] = found


def example_squares(tokens, deltas, precond, pub):
    quads, priv, cols = deltas.shape
    out = pl.pallas_call(
        lambda *refs: norms_kernel(pub, *refs),
        grid=(quads,),
        in_specs=[
            token_spec(tokens),
            pl.BlockSpec((1, priv, cols), lambda q: (q, 0, 0)),
            pl.BlockSpec(precond.shape, lambda q: (0, 0, 0)),
        ],
        out_specs=pl.BlockSpec((1, 8, L), lambda q: (q, 0, 0)),
        out_shape=jax.ShapeDtypeStruct((quads, 8, L), jnp.float32),
        name="example_squares",
    )(tokens, deltas, precond)
    return out[:, : priv // L, 0]


def clipped_kernel(pub, factors_ref, tokens_ref, delta_ref, out_ref, acc_ref):
    quad = pl.program_id(0)
    examples = delta_ref.shape[1] // L
    weighted = jnp.concatenate(
        [
            (
                factors_ref[quad, example]
                * delta_ref[0, example * L : (example + 1) * L, :].astype(jnp.float32)
            ).astype(jnp.bfloat16)
            for example in range(examples)
        ],
        axis=0,
    )

    @pl.when(quad == 0)
    def _():
        acc_ref[...] = jnp.zeros_like(acc_ref)

    for side, (b, h) in enumerate(token_sides(tokens_ref)):
        acc_ref[side] += jnp.dot(
            tokens_ref[b, 0, h, :, pub:], weighted, preferred_element_type=jnp.float32
        )

    @pl.when(quad == pl.num_programs(0) - 1)
    def _():
        out_ref[...] = acc_ref[...].astype(out_ref.dtype)


def clipped_sum(factors, tokens, deltas, pub):
    cores, quads, halves, rows, span = tokens.shape
    priv, cols = deltas.shape[1:]
    whole = (cores * halves, rows, cols)
    return pl.pallas_call(
        lambda *refs: clipped_kernel(pub, *refs),
        grid=(quads,),
        in_specs=[
            pl.BlockSpec(memory_space=pltpu.SMEM),
            token_spec(tokens),
            pl.BlockSpec((1, priv, cols), lambda q: (q, 0, 0)),
        ],
        out_specs=pl.BlockSpec(whole, lambda q: (0, 0, 0)),
        out_shape=jax.ShapeDtypeStruct(whole, jnp.bfloat16),
        scratch_shapes=[pltpu.VMEM(whole, jnp.float32)],
        name="clipped_sum",
    )(factors, tokens, deltas)


def gather_tokens(own, replicas):
    chips = replicas // CORES
    z = lax.div(lax.axis_index("replica"), CORES)
    up = [(r, (r + CORES) % replicas) for r in range(replicas)]
    down = [(r, (r - CORES) % replicas) for r in range(replicas)]
    swap = [(r, r ^ 1) for r in range(replicas)]
    held = jnp.zeros((CORES, chips, *own.shape), own.dtype)

    def place(held, block, chip):
        pair = jnp.stack([block, lax.ppermute(block, "replica", swap)])[:, None]
        return lax.dynamic_update_slice(held, pair, (0, lax.rem(chip, chips), 0, 0))

    held = place(held, own, z)
    below, above = own, own
    for step in range(1, chips // 2):
        below = lax.ppermute(below, "replica", up)
        above = lax.ppermute(above, "replica", down)
        held = place(held, below, z + chips - step)
        held = place(held, above, z + step)
    half = own.shape[0] // 2
    last = jnp.concatenate(
        [
            lax.ppermute(below[:half], "replica", up),
            lax.ppermute(above[half:], "replica", down),
        ],
        axis=0,
    )
    held = place(held, last, z + chips // 2)
    return held.reshape(CORES, chips // 2, 2, *own.shape)


def on_device(
    public_tokens,
    public_targets,
    private_tokens,
    private_targets,
    token_counts,
    weight,
    public_moment,
    adam_first,
    adam_second,
    noise_draw,
):
    replicas = lax.axis_size("replica")
    along_x = [[x * SIDE + y for x in range(SIDE)] for y in range(SIDE)]
    along_y = [[x * SIDE + y for y in range(SIDE)] for x in range(SIDE)]
    quads = replicas // SIDE
    pub = public_tokens.shape[0]
    priv = private_tokens.shape[0]
    cols = weight.shape[1]
    examples_here = token_counts.shape[1]
    pub_rows = public_targets.shape[0]
    priv_rows = private_targets.shape[0]
    moves = to_class(replicas)

    live = (
        jnp.arange(L, dtype=jnp.int32)[None, :] < token_counts[0][:, None]
    ).reshape(priv)
    live_tokens = jnp.where(live[:, None], private_tokens, jnp.zeros_like(private_tokens))
    local = jnp.concatenate([public_tokens.T, live_tokens.T], axis=1)
    local = lax.ppermute(local, ("replica", "tile"), moves)
    tokens = gather_tokens(local, replicas)
    core = lax.rem(lax.axis_index("replica"), CORES)

    def own_core_first(sides):
        split = sides.reshape(2, CORES, *sides.shape[1:])
        split = jnp.where(core == 0, split, split[:, ::-1])
        return split.transpose(1, 0, 2, 3).reshape(sides.shape)

    def by_side(mine):
        split = mine.reshape(CORES, 2, *mine.shape[1:])
        split = jnp.where(core == 0, split, split[::-1])
        return split.transpose(1, 0, 2, 3).reshape(mine.shape)

    w_half = weight.astype(jnp.bfloat16)
    w_group = own_core_first(
        lax.all_to_all(
            everywhere(w_half, SIDE), "tile", 0, 0, tiled=True, axis_index_groups=along_x
        )
    )

    spans = (pub_rows, priv_rows)
    chunk = SIDE * (pub_rows + priv_rows)
    targets = jnp.concatenate([public_targets, private_targets], axis=0)
    targets = lax.ppermute(targets, ("replica", "tile"), moves)
    targets = targets.reshape(-1, replicas, cols).transpose(1, 0, 2)
    targets = lax.all_to_all(targets, "replica", 0, 0, tiled=True)
    targets = targets.reshape(quads, SIDE, pub_rows + priv_rows, cols)
    targets = jnp.concatenate(
        [
            targets[:, :, :pub_rows].reshape(quads, SIDE * pub_rows, cols),
            targets[:, :, pub_rows:].reshape(quads, SIDE * priv_rows, cols),
        ],
        axis=1,
    ).reshape(quads * chunk, cols)

    sent = outputs_by_owner(tokens, w_group, pub, spans).reshape(SIDE, quads * chunk, cols)
    got, (targets, tokens) = exchange(sent, "tile", along_y, (targets, tokens))
    total = jnp.sum(got.astype(jnp.float32), axis=0)
    delta = (total - targets.astype(jnp.float32)).astype(jnp.bfloat16)
    deltas, (tokens, public_moment) = exchange(
        everywhere(delta, SIDE), "tile", along_y, (tokens, public_moment)
    )

    def over_classes(part):
        got, _ = exchange(by_side(part), "tile", along_x)
        return jnp.sum(got.astype(jnp.float32), axis=0)

    product, private_delta = public_product(
        tokens, deltas.reshape(SIDE, quads, chunk, cols), pub, spans
    )
    public_grad = over_classes(product) / math.sqrt(pub * replicas)
    new_public = beta_public * public_moment + (1.0 - beta_public) * public_grad * public_grad
    precond = 1.0 / (jnp.sqrt(new_public) + public_epsilon)
    precond_group, _ = exchange(
        everywhere(precond.astype(jnp.bfloat16), SIDE), "tile", along_x
    )

    squares = example_squares(tokens, private_delta, own_core_first(precond_group), pub)
    squares = jnp.sum(exchange(everywhere(squares, SIDE), "tile", along_y)[0], axis=0)
    squares = jnp.sum(exchange(everywhere(squares, replicas), "replica", None)[0], axis=0)
    clip_norm = clip_factor * math.sqrt(L * D * Q)
    factors = clip_norm / jnp.maximum(jnp.sqrt(squares), clip_norm)
    summed = precond * over_classes(clipped_sum(factors, tokens, private_delta, pub))

    examples_total = examples_here * replicas
    noise_scale = noise_level * clip_factor * math.sqrt(L)
    gradient = (summed + noise_scale * noise_draw) / examples_total
    new_first = beta_first * adam_first + (1.0 - beta_first) * gradient
    new_second = beta_second * adam_second + (1.0 - beta_second) * gradient * gradient
    first_hat = new_first / (1.0 - beta_first**2)
    second_hat = new_second / (1.0 - beta_second**2)
    new_weight = weight - learn_rate * first_hat / (jnp.sqrt(second_hat) + adam_epsilon)
    return (new_weight, new_first, new_second, new_public)


def solution(mesh):
    placed = (
        P("replica", "tile"),
        P(("replica", "tile"), None),
        P("replica", "tile"),
        P(("replica", "tile"), None),
        P("replica", None),
        P("tile", "replica"),
        P("tile", "replica"),
        P("tile", "replica"),
        P("tile", "replica"),
        P("tile", "replica"),
    )
    return jax.shard_map(
        on_device,
        mesh=mesh,
        in_specs=placed,
        out_specs=(
            P("tile", "replica"),
            P("tile", "replica"),
            P("tile", "replica"),
            P("tile", "replica"),
        ),
        check_vma=False,
    )
```

```python
import math

import jax
import jax.numpy as jnp
from jax import lax
from jax.experimental import pallas as pl
from jax.experimental.pallas import tpu as pltpu
from jax.sharding import PartitionSpec as P

D = 5120
L = 128
Q = 4096
CORES = 2
SIDE = 4
LANES = 128


beta_first = 0.9
beta_second = 0.99
beta_public = 0.9
public_epsilon = 0.001
adam_epsilon = 1e-08
clip_factor = 0.6
noise_level = 4.0
learn_rate = 0.01


def exchange(sent, axis, groups, kept=()):
    sent, kept = lax.optimization_barrier((sent, kept))
    got = lax.all_to_all(sent, axis, 0, 0, tiled=True, axis_index_groups=groups)
    return lax.optimization_barrier((got, kept))


def everywhere(values, parts):
    return jnp.broadcast_to(values[None], (parts, *values.shape))


def to_class(replicas):
    tiles = SIDE * SIDE
    moves = []
    for replica in range(replicas):
        quad, inner = divmod(replica, CORES * 2)
        odd, core = divmod(inner, CORES)
        for tile in range(tiles):
            x, y = divmod(tile, SIDE)
            target = (quad * SIDE + x) * tiles + (odd + 2 * core) * SIDE + y
            moves.append((replica * tiles + tile, target))
    return moves


def token_sides(tokens_ref):
    return [(b, h) for b in range(tokens_ref.shape[0]) for h in range(tokens_ref.shape[2])]


def token_spec(tokens, lanes, at=0):
    cores, _, halves, rows, _ = tokens.shape
    return pl.BlockSpec((cores, 1, halves, rows, lanes), lambda q: (0, q, 0, 0, at))


def outputs_kernel(priv, spans, tokens_ref, w_ref, out_ref):
    span = tokens_ref.shape[4]
    total = jnp.zeros((span, w_ref.shape[2]), jnp.float32)
    for side, (b, h) in enumerate(token_sides(tokens_ref)):
        total = total + lax.dot_general(
            tokens_ref[b, 0, h],
            w_ref[side],
            (((0,), (0,)), ((), ())),
            preferred_element_type=jnp.float32,
        )
    for owner in range(SIDE):
        pieces = []
        for first, rows in ((priv, spans[0]), (0, spans[1])):
            for x in range(SIDE):
                at = first + (x * SIDE + owner) * rows
                pieces.append(total[at : at + rows])
        owned = jnp.concatenate(pieces, axis=0).astype(out_ref.dtype)
        for part in range(out_ref.shape[2]):
            out_ref[owner, 0, part] = owned[:, part * LANES : (part + 1) * LANES]


def outputs_by_owner(tokens, w_group, priv, spans):
    quads = tokens.shape[1]
    chunk, cols = SIDE * sum(spans), w_group.shape[2]
    block = (SIDE, 1, cols // LANES, chunk, LANES)
    return pl.pallas_call(
        lambda *refs: outputs_kernel(priv, spans, *refs),
        grid=(quads,),
        in_specs=[
            token_spec(tokens, tokens.shape[4]),
            pl.BlockSpec(w_group.shape, lambda q: (0, 0, 0)),
        ],
        out_specs=pl.BlockSpec(block, lambda q: (0, q, 0, 0, 0)),
        out_shape=jax.ShapeDtypeStruct((SIDE, quads, *block[2:]), jnp.bfloat16),
        name="outputs_by_owner",
    )(tokens, w_group)


def public_kernel(spans, low_ref, high_ref, deltas_ref, out_ref, private_ref, acc_ref):
    quad = pl.program_id(0)
    parts = deltas_ref.shape[2]
    deltas = jnp.concatenate([deltas_ref[:, 0, part] for part in range(parts)], axis=-1)
    deltas = deltas.astype(jnp.float32)
    ordered = []
    for first, rows in ((0, spans[0]), (SIDE * spans[0], spans[1])):
        pieces = [
            deltas[owner, first + x * rows : first + (x + 1) * rows]
            for x in range(SIDE)
            for owner in range(SIDE)
        ]
        ordered.append(jnp.concatenate(pieces, axis=0).astype(jnp.bfloat16))
    private_ref[0] = ordered[1]

    @pl.when(quad == 0)
    def _():
        acc_ref[...] = jnp.zeros_like(acc_ref)

    for side, (b, h) in enumerate(token_sides(low_ref)):
        block_x = jnp.concatenate([low_ref[b, 0, h], high_ref[b, 0, h]], axis=-1)
        acc_ref[side] += jnp.dot(block_x, ordered[0], preferred_element_type=jnp.float32)

    @pl.when(quad == pl.num_programs(0) - 1)
    def _():
        out_ref[...] = acc_ref[...].astype(out_ref.dtype)


def public_product(tokens, deltas, priv, spans):
    cores, quads, halves, rows, _ = tokens.shape
    parts, chunk = deltas.shape[2:4]
    whole = (cores * halves, rows, parts * LANES)
    return pl.pallas_call(
        lambda *refs: public_kernel(spans, *refs),
        grid=(quads,),
        in_specs=[
            token_spec(tokens, L, priv // L),
            token_spec(tokens, L, priv // L + 1),
            pl.BlockSpec((SIDE, 1, parts, chunk, LANES), lambda q: (0, q, 0, 0, 0)),
        ],
        out_specs=[
            pl.BlockSpec(whole, lambda q: (0, 0, 0)),
            pl.BlockSpec((1, priv, parts * LANES), lambda q: (q, 0, 0)),
        ],
        out_shape=[
            jax.ShapeDtypeStruct(whole, jnp.bfloat16),
            jax.ShapeDtypeStruct((quads, priv, parts * LANES), jnp.bfloat16),
        ],
        scratch_shapes=[pltpu.VMEM(whole, jnp.float32)],
        name="public_product",
    )(tokens, tokens, deltas)


def norms_kernel(tokens_ref, delta_ref, precond_ref, out_ref):
    rows = tokens_ref.shape[3]
    examples = delta_ref.shape[1] // L
    row_at = lax.broadcasted_iota(jnp.int32, out_ref.shape[1:], 0)
    found = jnp.zeros(out_ref.shape[1:], jnp.float32)
    for example in range(examples):
        block_d = delta_ref[0, example * L : (example + 1) * L, :]
        first = example * L
        acc = jnp.zeros((8, block_d.shape[1]), jnp.float32)
        for side, (b, h) in enumerate(token_sides(tokens_ref)):
            grads = jnp.dot(
                tokens_ref[b, 0, h, :, first : first + L],
                block_d,
                preferred_element_type=jnp.float32,
            )
            scaled = grads * precond_ref[side].astype(jnp.float32)
            acc = acc + jnp.sum((scaled * scaled).reshape(rows // 8, 8, -1), axis=0)
        found = jnp.where(row_at == example, jnp.sum(acc), found)
    out_ref[0] = found


def example_squares(tokens, deltas, precond):
    quads, priv, cols = deltas.shape
    out = pl.pallas_call(
        norms_kernel,
        grid=(quads,),
        in_specs=[
            token_spec(tokens, priv),
            pl.BlockSpec((1, priv, cols), lambda q: (q, 0, 0)),
            pl.BlockSpec(precond.shape, lambda q: (0, 0, 0)),
        ],
        out_specs=pl.BlockSpec((1, 8, L), lambda q: (q, 0, 0)),
        out_shape=jax.ShapeDtypeStruct((quads, 8, L), jnp.float32),
        name="example_squares",
    )(tokens, deltas, precond)
    return out[:, : priv // L, 0]


def clipped_kernel(factors_ref, tokens_ref, delta_ref, out_ref, acc_ref):
    quad = pl.program_id(0)
    examples = delta_ref.shape[1] // L
    weighted = jnp.concatenate(
        [
            (
                factors_ref[quad, example]
                * delta_ref[0, example * L : (example + 1) * L, :].astype(jnp.float32)
            ).astype(jnp.bfloat16)
            for example in range(examples)
        ],
        axis=0,
    )

    @pl.when(quad == 0)
    def _():
        acc_ref[...] = jnp.zeros_like(acc_ref)

    for side, (b, h) in enumerate(token_sides(tokens_ref)):
        acc_ref[side] += jnp.dot(
            tokens_ref[b, 0, h], weighted, preferred_element_type=jnp.float32
        )

    @pl.when(quad == pl.num_programs(0) - 1)
    def _():
        out_ref[...] = acc_ref[...].astype(out_ref.dtype)


def clipped_sum(factors, tokens, deltas):
    cores, quads, halves, rows, _ = tokens.shape
    priv, cols = deltas.shape[1:]
    whole = (cores * halves, rows, cols)
    return pl.pallas_call(
        clipped_kernel,
        grid=(quads,),
        in_specs=[
            pl.BlockSpec(memory_space=pltpu.SMEM),
            token_spec(tokens, priv),
            pl.BlockSpec((1, priv, cols), lambda q: (q, 0, 0)),
        ],
        out_specs=pl.BlockSpec(whole, lambda q: (0, 0, 0)),
        out_shape=jax.ShapeDtypeStruct(whole, jnp.bfloat16),
        scratch_shapes=[pltpu.VMEM(whole, jnp.float32)],
        name="clipped_sum",
    )(factors, tokens, deltas)


def gather_tokens(own, moves, replicas, state, jobs):
    chips = replicas // CORES
    z = lax.div(lax.axis_index("replica"), CORES)
    up = [(r, (r + CORES) % replicas) for r in range(replicas)]
    down = [(r, (r - CORES) % replicas) for r in range(replicas)]
    swap = [(r, r ^ 1) for r in range(replicas)]
    held = jnp.zeros((CORES, chips, *own.shape), own.dtype)

    def swapped(block):
        return jnp.stack([block, lax.ppermute(block, "replica", swap)])[:, None]

    def place(held, pair, chip):
        return lax.dynamic_update_slice(held, pair, (0, lax.rem(chip, chips), 0, 0))

    own = lax.ppermute(own, ("replica", "tile"), moves)
    state = jobs[0](state)
    own, held, state = lax.optimization_barrier((own, held, state))
    below, above = own, own
    waiting = [(swapped(own), z)]
    for step in range(1, chips // 2):
        below = lax.ppermute(below, "replica", up)
        above = lax.ppermute(above, "replica", down)
        for pair, chip in waiting:
            held = place(held, pair, chip)
        state = jobs[step](state)
        below, above, held, state = lax.optimization_barrier((below, above, held, state))
        waiting = [
            (swapped(below), z + chips - step),
            (swapped(above), z + step),
        ]
    half = own.shape[0] // 2
    low = lax.ppermute(below[:half], "replica", up)
    high = lax.ppermute(above[half:], "replica", down)
    for pair, chip in waiting:
        held = place(held, pair, chip)
    low, high, held, state = lax.optimization_barrier((low, high, held, state))
    last = jnp.concatenate([low, high], axis=0)
    held = place(held, swapped(last), z + chips // 2)
    return held.reshape(CORES, chips // 2, 2, *own.shape), state


def on_device(
    public_tokens,
    public_targets,
    private_tokens,
    private_targets,
    token_counts,
    weight,
    public_moment,
    adam_first,
    adam_second,
    noise_draw,
):
    replicas = lax.axis_size("replica")
    along_x = [[x * SIDE + y for x in range(SIDE)] for y in range(SIDE)]
    along_y = [[x * SIDE + y for y in range(SIDE)] for x in range(SIDE)]
    quads = replicas // SIDE
    pub = public_tokens.shape[0]
    priv = private_tokens.shape[0]
    cols = weight.shape[1]
    examples_here = token_counts.shape[1]
    pub_rows = public_targets.shape[0]
    priv_rows = private_targets.shape[0]
    moves = to_class(replicas)

    live = (
        jnp.arange(L, dtype=jnp.int32)[None, :] < token_counts[0][:, None]
    ).reshape(priv)
    live_tokens = jnp.where(live[:, None], private_tokens, jnp.zeros_like(private_tokens))
    local = jnp.concatenate([live_tokens.T, public_tokens.T], axis=1)
    core = lax.rem(lax.axis_index("replica"), CORES)
    parts = cols // LANES
    spans = (pub_rows, priv_rows)
    chunk = SIDE * (pub_rows + priv_rows)

    def own_core_first(sides):
        split = sides.reshape(2, CORES, *sides.shape[1:])
        split = jnp.where(core == 0, split, split[:, ::-1])
        return split.transpose(1, 0, 2, 3).reshape(sides.shape)

    def by_side(mine):
        split = mine.reshape(CORES, 2, *mine.shape[1:])
        split = jnp.where(core == 0, split, split[::-1])
        return split.transpose(1, 0, 2, 3).reshape(mine.shape)

    def across_x(sent):
        return lax.all_to_all(sent, "tile", 0, 0, tiled=True, axis_index_groups=along_x)

    def targets_to_columns(state):
        targets, w_half = state
        return lax.all_to_all(targets, "replica", 0, 0, tiled=True), w_half

    def targets_to_class(state):
        targets, w_half = state
        targets = targets.reshape(quads, 2, CORES, -1, cols).transpose(2, 1, 0, 3, 4)
        return across_x(targets.reshape(SIDE, -1, cols)), w_half

    def weight_to_group(state):
        targets, w_half = state
        return targets, across_x(everywhere(w_half, SIDE))

    def arranged(state):
        targets, w_group = state
        targets = targets.reshape(SIDE, quads, pub_rows + priv_rows, cols).transpose(1, 0, 2, 3)
        targets = jnp.concatenate(
            [
                targets[:, :, :pub_rows].reshape(quads, SIDE * pub_rows, cols),
                targets[:, :, pub_rows:].reshape(quads, SIDE * priv_rows, cols),
            ],
            axis=1,
        )
        halves = [targets[:, None, :, p * LANES : (p + 1) * LANES] for p in range(parts)]
        targets = jnp.concatenate(halves, axis=1).reshape(quads * parts * chunk, LANES)
        return targets, own_core_first(w_group)

    targets = jnp.concatenate([public_targets, private_targets], axis=0)
    targets = targets.reshape(-1, replicas, cols).transpose(1, 0, 2)
    tokens, (targets, w_group) = gather_tokens(
        local,
        moves,
        replicas,
        (targets, weight.astype(jnp.bfloat16)),
        [targets_to_columns, targets_to_class, weight_to_group, arranged],
    )

    sent = outputs_by_owner(tokens, w_group, priv, spans).reshape(SIDE, -1, LANES)
    got, (targets, tokens) = exchange(sent, "tile", along_y, (targets, tokens))
    total = jnp.sum(got.astype(jnp.float32), axis=0)
    delta = (total - targets.astype(jnp.float32)).astype(jnp.bfloat16)
    deltas, (tokens, public_moment) = exchange(
        everywhere(delta, SIDE), "tile", along_y, (tokens, public_moment)
    )

    def over_classes(part):
        got, _ = exchange(by_side(part), "tile", along_x)
        return jnp.sum(got.astype(jnp.float32), axis=0)

    product, private_delta = public_product(
        tokens, deltas.reshape(SIDE, quads, parts, chunk, LANES), priv, spans
    )
    public_grad = over_classes(product) / math.sqrt(pub * replicas)
    new_public = beta_public * public_moment + (1.0 - beta_public) * public_grad * public_grad
    precond = 1.0 / (jnp.sqrt(new_public) + public_epsilon)
    precond_group, _ = exchange(
        everywhere(precond.astype(jnp.bfloat16), SIDE), "tile", along_x
    )

    squares = example_squares(tokens, private_delta, own_core_first(precond_group))
    squares = jnp.sum(exchange(everywhere(squares, SIDE), "tile", along_y)[0], axis=0)
    squares = jnp.sum(exchange(everywhere(squares, replicas), "replica", None)[0], axis=0)
    clip_norm = clip_factor * math.sqrt(L * D * Q)
    factors = clip_norm / jnp.maximum(jnp.sqrt(squares), clip_norm)
    summed = precond * over_classes(clipped_sum(factors, tokens, private_delta))

    examples_total = examples_here * replicas
    noise_scale = noise_level * clip_factor * math.sqrt(L)
    gradient = (summed + noise_scale * noise_draw) / examples_total
    new_first = beta_first * adam_first + (1.0 - beta_first) * gradient
    new_second = beta_second * adam_second + (1.0 - beta_second) * gradient * gradient
    first_hat = new_first / (1.0 - beta_first**2)
    second_hat = new_second / (1.0 - beta_second**2)
    new_weight = weight - learn_rate * first_hat / (jnp.sqrt(second_hat) + adam_epsilon)
    return (new_weight, new_first, new_second, new_public)


def solution(mesh):
    placed = (
        P("replica", "tile"),
        P(("replica", "tile"), None),
        P("replica", "tile"),
        P(("replica", "tile"), None),
        P("replica", None),
        P("tile", "replica"),
        P("tile", "replica"),
        P("tile", "replica"),
        P("tile", "replica"),
        P("tile", "replica"),
    )
    return jax.shard_map(
        on_device,
        mesh=mesh,
        in_specs=placed,
        out_specs=(
            P("tile", "replica"),
            P("tile", "replica"),
            P("tile", "replica"),
            P("tile", "replica"),
        ),
        check_vma=False,
    )
```

```python
import math

import jax
import jax.numpy as jnp
from jax import lax
from jax.experimental import pallas as pl
from jax.experimental.pallas import tpu as pltpu
from jax.sharding import PartitionSpec as P

D = 5120
L = 128
Q = 4096
CORES = 2
SIDE = 4


beta_first = 0.9
beta_second = 0.99
beta_public = 0.9
public_epsilon = 0.001
adam_epsilon = 1e-08
clip_factor = 0.6
noise_level = 4.0
learn_rate = 0.01


def exchange(sent, axis, groups, kept=()):
    sent, kept = lax.optimization_barrier((sent, kept))
    got = lax.all_to_all(sent, axis, 0, 0, tiled=True, axis_index_groups=groups)
    return lax.optimization_barrier((got, kept))


def everywhere(values, parts):
    return jnp.broadcast_to(values[None], (parts, *values.shape))


def to_class(replicas):
    tiles = SIDE * SIDE
    moves = []
    for replica in range(replicas):
        quad, inner = divmod(replica, CORES * 2)
        odd, core = divmod(inner, CORES)
        for tile in range(tiles):
            x, y = divmod(tile, SIDE)
            target = (quad * SIDE + x) * tiles + (odd + 2 * core) * SIDE + y
            moves.append((replica * tiles + tile, target))
    return moves


def norms_kernel(tokens_ref, delta_ref, precond_ref, out_ref):
    sides, rows = tokens_ref.shape[1], tokens_ref.shape[2]
    examples = delta_ref.shape[1] // L
    row_at = lax.broadcasted_iota(jnp.int32, out_ref.shape[1:], 0)
    found = jnp.zeros(out_ref.shape[1:], jnp.float32)
    for example in range(examples):
        block_d = delta_ref[0, example * L : (example + 1) * L, :]
        first = example * L
        acc = jnp.zeros((8, block_d.shape[1]), jnp.float32)
        for side in range(sides):
            grads = jnp.dot(
                tokens_ref[0, side, :, first : first + L],
                block_d,
                preferred_element_type=jnp.float32,
            )
            scaled = grads * precond_ref[side].astype(jnp.float32)
            acc = acc + jnp.sum((scaled * scaled).reshape(rows // 8, 8, -1), axis=0)
        found = jnp.where(row_at == example, jnp.sum(acc), found)
    out_ref[0] = found


def example_squares(tokens, deltas, precond):
    quads, sides, rows, _ = tokens.shape
    priv, cols = deltas.shape[1:]
    out = pl.pallas_call(
        norms_kernel,
        grid=(quads,),
        in_specs=[
            pl.BlockSpec((1, sides, rows, priv), lambda q: (q, 0, 0, 0)),
            pl.BlockSpec((1, priv, cols), lambda q: (q, 0, 0)),
            pl.BlockSpec((sides, rows, cols), lambda q: (0, 0, 0)),
        ],
        out_specs=pl.BlockSpec((1, 8, L), lambda q: (q, 0, 0)),
        out_shape=jax.ShapeDtypeStruct((quads, 8, L), jnp.float32),
        name="example_squares",
    )(tokens, deltas, precond)
    return out[:, : priv // L, 0]


def clipped_kernel(factors_ref, tokens_ref, delta_ref, out_ref, acc_ref):
    quad = pl.program_id(0)
    examples = delta_ref.shape[1] // L
    weighted = jnp.concatenate(
        [
            (
                factors_ref[quad, example]
                * delta_ref[0, example * L : (example + 1) * L, :].astype(jnp.float32)
            ).astype(jnp.bfloat16)
            for example in range(examples)
        ],
        axis=0,
    )

    @pl.when(quad == 0)
    def _():
        acc_ref[...] = jnp.zeros_like(acc_ref)

    for side in range(tokens_ref.shape[1]):
        acc_ref[side] += jnp.dot(
            tokens_ref[0, side], weighted, preferred_element_type=jnp.float32
        )

    @pl.when(quad == pl.num_programs(0) - 1)
    def _():
        out_ref[...] = acc_ref[...].astype(out_ref.dtype)


def clipped_sum(factors, tokens, deltas):
    quads, sides, rows, _ = tokens.shape
    priv, cols = deltas.shape[1:]
    return pl.pallas_call(
        clipped_kernel,
        grid=(quads,),
        in_specs=[
            pl.BlockSpec(memory_space=pltpu.SMEM),
            pl.BlockSpec((1, sides, rows, priv), lambda q: (q, 0, 0, 0)),
            pl.BlockSpec((1, priv, cols), lambda q: (q, 0, 0)),
        ],
        out_specs=pl.BlockSpec((sides, rows, cols), lambda q: (0, 0, 0)),
        out_shape=jax.ShapeDtypeStruct((sides, rows, cols), jnp.bfloat16),
        scratch_shapes=[pltpu.VMEM((sides, rows, cols), jnp.float32)],
        name="clipped_sum",
    )(factors, tokens, deltas)


def on_device(
    public_tokens,
    public_targets,
    private_tokens,
    private_targets,
    token_counts,
    weight,
    public_moment,
    adam_first,
    adam_second,
    noise_draw,
):
    replicas = lax.axis_size("replica")
    along_x = [[x * SIDE + y for x in range(SIDE)] for y in range(SIDE)]
    along_y = [[x * SIDE + y for y in range(SIDE)] for x in range(SIDE)]
    same_class = [
        [r * SIDE * SIDE + x * SIDE + y for r in range(replicas) for y in range(SIDE)]
        for x in range(SIDE)
    ]
    quads = replicas // SIDE
    pub = public_tokens.shape[0]
    priv = private_tokens.shape[0]
    rows, cols = weight.shape
    examples_here = token_counts.shape[1]
    pub_rows = public_targets.shape[0]
    priv_rows = private_targets.shape[0]
    pub_all = quads * SIDE * pub_rows
    priv_all = quads * SIDE * priv_rows
    moves = to_class(replicas)

    live = (
        jnp.arange(L, dtype=jnp.int32)[None, :] < token_counts[0][:, None]
    ).reshape(priv)
    live_tokens = jnp.where(live[:, None], private_tokens, jnp.zeros_like(private_tokens))
    local = jnp.concatenate([live_tokens.T, public_tokens.T], axis=1)
    def across_x(sent):
        return lax.all_to_all(sent, "tile", 0, 0, tiled=True, axis_index_groups=along_x)

    targets = jnp.concatenate([public_targets, private_targets], axis=0)
    targets = targets.reshape(-1, replicas, cols).transpose(1, 0, 2)
    local = lax.ppermute(local, ("replica", "tile"), moves)
    targets = lax.all_to_all(targets, "replica", 0, 0, tiled=True)
    w_half = weight.astype(jnp.bfloat16)
    local, targets, w_half = lax.optimization_barrier((local, targets, w_half))

    tokens = lax.all_gather(local, "replica", axis=0)
    tokens = tokens.reshape(quads, SIDE, rows, pub + priv)

    targets = targets.reshape(quads, 2, CORES, -1, cols).transpose(2, 1, 0, 3, 4)
    targets = across_x(targets.reshape(SIDE, -1, cols))
    w_group = across_x(everywhere(w_half, SIDE))
    targets = targets.reshape(SIDE, quads, pub_rows + priv_rows, cols).transpose(1, 0, 2, 3)
    targets = jnp.concatenate(
        [
            targets[:, :, :pub_rows].reshape(pub_all, cols),
            targets[:, :, pub_rows:].reshape(priv_all, cols),
        ],
        axis=0,
    )

    def by_owner(part, span):
        part = part.reshape(quads, SIDE, SIDE, span, cols)
        return part.transpose(2, 0, 1, 3, 4).reshape(SIDE, quads * SIDE * span, cols)

    def by_token(part, span):
        part = part.reshape(SIDE, quads, SIDE, span, cols)
        return part.transpose(1, 2, 0, 3, 4).reshape(quads, SIDE * SIDE * span, cols)

    out = jnp.einsum(
        "qxfn,xfk->qnk", tokens, w_group, preferred_element_type=jnp.float32
    ).astype(jnp.bfloat16)
    sent = jnp.concatenate(
        [by_owner(out[:, priv:], pub_rows), by_owner(out[:, :priv], priv_rows)], axis=1
    )
    got, (targets, tokens) = exchange(sent, "tile", along_y, (targets, tokens))
    total = jnp.sum(got.astype(jnp.float32), axis=0)
    delta = (total - targets.astype(jnp.float32)).astype(jnp.bfloat16)
    deltas, (tokens, public_moment) = exchange(
        everywhere(delta, SIDE), "tile", along_y, (tokens, public_moment)
    )
    public_delta = by_token(deltas[:, :pub_all], pub_rows)
    private_delta = by_token(deltas[:, pub_all:], priv_rows)

    def over_classes(part):
        got, _ = exchange(part.astype(jnp.bfloat16), "tile", along_x)
        return jnp.sum(got.astype(jnp.float32), axis=0)

    public_grad = over_classes(
        jnp.einsum(
            "qxfn,qnk->xfk",
            tokens[:, :, :, priv:],
            public_delta,
            preferred_element_type=jnp.float32,
        )
    ) / math.sqrt(pub * replicas)
    new_public = beta_public * public_moment + (1.0 - beta_public) * public_grad * public_grad
    precond = 1.0 / (jnp.sqrt(new_public) + public_epsilon)
    precond_group, _ = exchange(
        everywhere(precond.astype(jnp.bfloat16), SIDE), "tile", along_x
    )

    squares = example_squares(tokens, private_delta, precond_group)
    peers = replicas * SIDE
    squares, _ = exchange(everywhere(squares, peers), ("replica", "tile"), same_class)
    squares = jnp.sum(squares, axis=0)
    clip_norm = clip_factor * math.sqrt(L * D * Q)
    factors = clip_norm / jnp.maximum(jnp.sqrt(squares), clip_norm)
    summed = precond * over_classes(clipped_sum(factors, tokens, private_delta))

    examples_total = examples_here * replicas
    noise_scale = noise_level * clip_factor * math.sqrt(L)
    gradient = (summed + noise_scale * noise_draw) / examples_total
    new_first = beta_first * adam_first + (1.0 - beta_first) * gradient
    new_second = beta_second * adam_second + (1.0 - beta_second) * gradient * gradient
    first_hat = new_first / (1.0 - beta_first**2)
    second_hat = new_second / (1.0 - beta_second**2)
    new_weight = weight - learn_rate * first_hat / (jnp.sqrt(second_hat) + adam_epsilon)
    return (new_weight, new_first, new_second, new_public)


def solution(mesh):
    placed = (
        P("replica", "tile"),
        P(("replica", "tile"), None),
        P("replica", "tile"),
        P(("replica", "tile"), None),
        P("replica", None),
        P("tile", "replica"),
        P("tile", "replica"),
        P("tile", "replica"),
        P("tile", "replica"),
        P("tile", "replica"),
    )
    return jax.shard_map(
        on_device,
        mesh=mesh,
        in_specs=placed,
        out_specs=(
            P("tile", "replica"),
            P("tile", "replica"),
            P("tile", "replica"),
            P("tile", "replica"),
        ),
        check_vma=False,
    )
```

```python
import math

import jax
import jax.numpy as jnp
from jax import lax
from jax.experimental import pallas as pl
from jax.experimental.pallas import tpu as pltpu
from jax.sharding import PartitionSpec as P

D = 5120
L = 128
Q = 4096
CORES = 2
SIDE = 4
KERNEL_VMEM = 58 * 2**20


beta_first = 0.9
beta_second = 0.99
beta_public = 0.9
public_epsilon = 0.001
adam_epsilon = 1e-08
clip_factor = 0.6
noise_level = 4.0
learn_rate = 0.01


def exchange(sent, axis, groups, kept=()):
    sent, kept = lax.optimization_barrier((sent, kept))
    got = lax.all_to_all(sent, axis, 0, 0, tiled=True, axis_index_groups=groups)
    return lax.optimization_barrier((got, kept))


def everywhere(values, parts):
    return jnp.broadcast_to(values[None], (parts, *values.shape))


def to_class(replicas):
    tiles = SIDE * SIDE
    moves = []
    for replica in range(replicas):
        quad, inner = divmod(replica, CORES * 2)
        odd, core = divmod(inner, CORES)
        for tile in range(tiles):
            x, y = divmod(tile, SIDE)
            target = (quad * SIDE + x) * tiles + (odd + 2 * core) * SIDE + y
            moves.append((replica * tiles + tile, target))
    return moves


def norms_kernel(tokens_ref, delta_ref, precond_ref, out_ref):
    sides, rows = tokens_ref.shape[1], tokens_ref.shape[2]
    quad = pl.program_id(0)
    examples = delta_ref.shape[1] // L
    row_at = lax.broadcasted_iota(jnp.int32, out_ref.shape[1:], 0)
    found = jnp.zeros(out_ref.shape[1:], jnp.float32)
    for example in range(examples):
        block_d = delta_ref[quad, example * L : (example + 1) * L, :]
        first = example * L
        acc = jnp.zeros((8, block_d.shape[1]), jnp.float32)
        for side in range(sides):
            grads = jnp.dot(
                tokens_ref[0, side, :, first : first + L],
                block_d,
                preferred_element_type=jnp.float32,
            )
            scaled = grads * precond_ref[side].astype(jnp.float32)
            acc = acc + jnp.sum((scaled * scaled).reshape(rows // 8, 8, -1), axis=0)
        found = jnp.where(row_at == example, jnp.sum(acc), found)
    out_ref[0] = found


def example_squares(tokens, deltas, precond):
    quads, sides, rows, _ = tokens.shape
    priv, cols = deltas.shape[1:]
    out = pl.pallas_call(
        norms_kernel,
        grid=(quads,),
        in_specs=[
            pl.BlockSpec((1, sides, rows, priv), lambda q: (q, 0, 0, 0)),
            pl.BlockSpec(memory_space=pltpu.VMEM),
            pl.BlockSpec(memory_space=pltpu.VMEM),
        ],
        out_specs=pl.BlockSpec((1, 8, L), lambda q: (q, 0, 0)),
        out_shape=jax.ShapeDtypeStruct((quads, 8, L), jnp.float32),
        compiler_params=pltpu.CompilerParams(vmem_limit_bytes=KERNEL_VMEM),
        name="example_squares",
    )(tokens, deltas, precond)
    return out[:, : priv // L, 0]


def clipped_kernel(factors_ref, tokens_ref, delta_ref, out_ref, acc_ref):
    quad = pl.program_id(0)
    examples = delta_ref.shape[1] // L
    weighted = jnp.concatenate(
        [
            (
                factors_ref[quad, example]
                * delta_ref[quad, example * L : (example + 1) * L, :].astype(jnp.float32)
            ).astype(jnp.bfloat16)
            for example in range(examples)
        ],
        axis=0,
    )

    @pl.when(quad == 0)
    def _():
        acc_ref[...] = jnp.zeros_like(acc_ref)

    for side in range(tokens_ref.shape[1]):
        acc_ref[side] += jnp.dot(
            tokens_ref[0, side], weighted, preferred_element_type=jnp.float32
        )

    @pl.when(quad == pl.num_programs(0) - 1)
    def _():
        out_ref[...] = acc_ref[...].astype(out_ref.dtype)


def clipped_sum(factors, tokens, deltas):
    quads, sides, rows, _ = tokens.shape
    priv, cols = deltas.shape[1:]
    return pl.pallas_call(
        clipped_kernel,
        grid=(quads,),
        in_specs=[
            pl.BlockSpec(memory_space=pltpu.SMEM),
            pl.BlockSpec((1, sides, rows, priv), lambda q: (q, 0, 0, 0)),
            pl.BlockSpec(memory_space=pltpu.VMEM),
        ],
        out_specs=pl.BlockSpec((sides, rows, cols), lambda q: (0, 0, 0)),
        out_shape=jax.ShapeDtypeStruct((sides, rows, cols), jnp.bfloat16),
        scratch_shapes=[pltpu.VMEM((sides, rows, cols), jnp.float32)],
        compiler_params=pltpu.CompilerParams(vmem_limit_bytes=KERNEL_VMEM),
        name="clipped_sum",
    )(factors, tokens, deltas)


def on_device(
    public_tokens,
    public_targets,
    private_tokens,
    private_targets,
    token_counts,
    weight,
    public_moment,
    adam_first,
    adam_second,
    noise_draw,
):
    replicas = lax.axis_size("replica")
    along_x = [[x * SIDE + y for x in range(SIDE)] for y in range(SIDE)]
    along_y = [[x * SIDE + y for y in range(SIDE)] for x in range(SIDE)]
    same_class = [
        [r * SIDE * SIDE + x * SIDE + y for r in range(replicas) for y in range(SIDE)]
        for x in range(SIDE)
    ]
    quads = replicas // SIDE
    pub = public_tokens.shape[0]
    priv = private_tokens.shape[0]
    rows, cols = weight.shape
    examples_here = token_counts.shape[1]
    pub_rows = public_targets.shape[0]
    priv_rows = private_targets.shape[0]
    pub_all = quads * SIDE * pub_rows
    priv_all = quads * SIDE * priv_rows
    moves = to_class(replicas)

    live = (
        jnp.arange(L, dtype=jnp.int32)[None, :] < token_counts[0][:, None]
    ).reshape(priv)
    live_tokens = jnp.where(live[:, None], private_tokens, jnp.zeros_like(private_tokens))
    local = jnp.concatenate([live_tokens.T, public_tokens.T], axis=1)
    def across_x(sent):
        return lax.all_to_all(sent, "tile", 0, 0, tiled=True, axis_index_groups=along_x)

    targets = jnp.concatenate([public_targets, private_targets], axis=0)
    targets = targets.reshape(-1, replicas, cols).transpose(1, 0, 2)
    local = lax.ppermute(local, ("replica", "tile"), moves)
    targets = lax.all_to_all(targets, "replica", 0, 0, tiled=True)
    w_half = weight.astype(jnp.bfloat16)

    tokens = lax.all_gather(local, "replica", axis=0)
    tokens = tokens.reshape(quads, SIDE, rows, pub + priv)

    targets = targets.reshape(quads, 2, CORES, -1, cols).transpose(2, 1, 0, 3, 4)
    targets = across_x(targets.reshape(SIDE, -1, cols))
    w_group = across_x(everywhere(w_half, SIDE))
    targets = targets.reshape(SIDE, quads, pub_rows + priv_rows, cols).transpose(1, 0, 2, 3)
    targets = jnp.concatenate(
        [
            targets[:, :, :pub_rows].reshape(pub_all, cols),
            targets[:, :, pub_rows:].reshape(priv_all, cols),
        ],
        axis=0,
    )

    def by_owner(part, span):
        part = part.reshape(quads, SIDE, SIDE, span, cols)
        return part.transpose(2, 0, 1, 3, 4).reshape(SIDE, quads * SIDE * span, cols)

    def by_token(part, span):
        part = part.reshape(SIDE, quads, SIDE, span, cols)
        return part.transpose(1, 2, 0, 3, 4).reshape(quads, SIDE * SIDE * span, cols)

    out = jnp.einsum(
        "qxfn,xfk->qnk", tokens, w_group, preferred_element_type=jnp.float32
    ).astype(jnp.bfloat16)
    sent = jnp.concatenate(
        [by_owner(out[:, priv:], pub_rows), by_owner(out[:, :priv], priv_rows)], axis=1
    )
    got, (targets, tokens) = exchange(sent, "tile", along_y, (targets, tokens))
    total = jnp.sum(got.astype(jnp.float32), axis=0)
    delta = (total - targets.astype(jnp.float32)).astype(jnp.bfloat16)
    deltas, (tokens, public_moment) = exchange(
        everywhere(delta, SIDE), "tile", along_y, (tokens, public_moment)
    )
    public_delta = by_token(deltas[:, :pub_all], pub_rows)
    private_delta = by_token(deltas[:, pub_all:], priv_rows)

    def over_classes(part):
        got, _ = exchange(part.astype(jnp.bfloat16), "tile", along_x)
        return jnp.sum(got.astype(jnp.float32), axis=0)

    public_grad = over_classes(
        jnp.einsum(
            "qxfn,qnk->xfk",
            tokens[:, :, :, priv:],
            public_delta,
            preferred_element_type=jnp.float32,
        )
    ) / math.sqrt(pub * replicas)
    new_public = beta_public * public_moment + (1.0 - beta_public) * public_grad * public_grad
    precond = 1.0 / (jnp.sqrt(new_public) + public_epsilon)
    precond_group, _ = exchange(
        everywhere(precond.astype(jnp.bfloat16), SIDE), "tile", along_x
    )

    squares = example_squares(tokens, private_delta, precond_group)
    peers = replicas * SIDE
    squares, _ = exchange(everywhere(squares, peers), ("replica", "tile"), same_class)
    squares = jnp.sum(squares, axis=0)
    clip_norm = clip_factor * math.sqrt(L * D * Q)
    factors = clip_norm / jnp.maximum(jnp.sqrt(squares), clip_norm)
    summed = precond * over_classes(clipped_sum(factors, tokens, private_delta))

    examples_total = examples_here * replicas
    noise_scale = noise_level * clip_factor * math.sqrt(L)
    gradient = (summed + noise_scale * noise_draw) / examples_total
    new_first = beta_first * adam_first + (1.0 - beta_first) * gradient
    new_second = beta_second * adam_second + (1.0 - beta_second) * gradient * gradient
    first_hat = new_first / (1.0 - beta_first**2)
    second_hat = new_second / (1.0 - beta_second**2)
    new_weight = weight - learn_rate * first_hat / (jnp.sqrt(second_hat) + adam_epsilon)
    return (new_weight, new_first, new_second, new_public)


def solution(mesh):
    placed = (
        P("replica", "tile"),
        P(("replica", "tile"), None),
        P("replica", "tile"),
        P(("replica", "tile"), None),
        P("replica", None),
        P("tile", "replica"),
        P("tile", "replica"),
        P("tile", "replica"),
        P("tile", "replica"),
        P("tile", "replica"),
    )
    return jax.shard_map(
        on_device,
        mesh=mesh,
        in_specs=placed,
        out_specs=(
            P("tile", "replica"),
            P("tile", "replica"),
            P("tile", "replica"),
            P("tile", "replica"),
        ),
        check_vma=False,
    )
```

```python
import math

import jax
import jax.numpy as jnp
from jax import lax
from jax.experimental import pallas as pl
from jax.experimental.pallas import tpu as pltpu
from jax.sharding import PartitionSpec as P

D = 5120
L = 128
Q = 4096
CORES = 2
SIDE = 4
KERNEL_VMEM = 58 * 2**20


beta_first = 0.9
beta_second = 0.99
beta_public = 0.9
public_epsilon = 0.001
adam_epsilon = 1e-08
clip_factor = 0.6
noise_level = 4.0
learn_rate = 0.01


def exchange(sent, axis, groups, kept=()):
    sent, kept = lax.optimization_barrier((sent, kept))
    got = lax.all_to_all(sent, axis, 0, 0, tiled=True, axis_index_groups=groups)
    return lax.optimization_barrier((got, kept))


def everywhere(values, parts):
    return jnp.broadcast_to(values[None], (parts, *values.shape))


def to_class(replicas):
    tiles = SIDE * SIDE
    moves = []
    for replica in range(replicas):
        quad, inner = divmod(replica, CORES * 2)
        odd, core = divmod(inner, CORES)
        for tile in range(tiles):
            x, y = divmod(tile, SIDE)
            target = (quad * SIDE + x) * tiles + (odd + 2 * core) * SIDE + y
            moves.append((replica * tiles + tile, target))
    return moves


def live_kernel(counts_ref, private_ref, public_ref, out_ref):
    rows, priv = private_ref.shape
    slot = lax.broadcasted_iota(jnp.int32, (rows, L), 1)
    for example in range(priv // L):
        lanes = slice(example * L, (example + 1) * L)
        block = private_ref[:, lanes].astype(jnp.float32)
        block = jnp.where(slot < counts_ref[0, example], block, 0.0)
        out_ref[:, lanes] = block.astype(out_ref.dtype)
    out_ref[:, priv:] = public_ref[...]


def live_block(counts, private, public):
    return pl.pallas_call(
        live_kernel,
        in_specs=[
            pl.BlockSpec(memory_space=pltpu.SMEM),
            pl.BlockSpec(memory_space=pltpu.VMEM),
            pl.BlockSpec(memory_space=pltpu.VMEM),
        ],
        out_specs=pl.BlockSpec(memory_space=pltpu.VMEM),
        out_shape=jax.ShapeDtypeStruct(
            (private.shape[0], private.shape[1] + public.shape[1]), private.dtype
        ),
        name="live_block",
    )(counts, private, public)


def norms_kernel(tokens_ref, delta_ref, precond_ref, out_ref, wide_ref):
    sides, rows = tokens_ref.shape[1], tokens_ref.shape[2]
    quad = pl.program_id(0)

    @pl.when(quad == 0)
    def _():
        wide_ref[...] = precond_ref[...].astype(jnp.float32)

    examples = delta_ref.shape[1] // L
    row_at = lax.broadcasted_iota(jnp.int32, out_ref.shape[1:], 0)
    found = jnp.zeros(out_ref.shape[1:], jnp.float32)
    for example in range(examples):
        block_d = delta_ref[quad, example * L : (example + 1) * L, :]
        first = example * L
        acc = jnp.zeros((8, block_d.shape[1]), jnp.float32)
        for side in range(sides):
            grads = jnp.dot(
                tokens_ref[0, side, :, first : first + L],
                block_d,
                preferred_element_type=jnp.float32,
            )
            scaled = grads * wide_ref[side]
            acc = acc + jnp.sum((scaled * scaled).reshape(rows // 8, 8, -1), axis=0)
        found = jnp.where(row_at == example, jnp.sum(acc), found)
    out_ref[0] = found


def example_squares(tokens, deltas, precond):
    quads, sides, rows, _ = tokens.shape
    priv, cols = deltas.shape[1:]
    out = pl.pallas_call(
        norms_kernel,
        grid=(quads,),
        in_specs=[
            pl.BlockSpec((1, sides, rows, priv), lambda q: (q, 0, 0, 0)),
            pl.BlockSpec(memory_space=pltpu.VMEM),
            pl.BlockSpec(memory_space=pltpu.VMEM),
        ],
        out_specs=pl.BlockSpec((1, 8, L), lambda q: (q, 0, 0)),
        out_shape=jax.ShapeDtypeStruct((quads, 8, L), jnp.float32),
        scratch_shapes=[pltpu.VMEM(precond.shape, jnp.float32)],
        compiler_params=pltpu.CompilerParams(vmem_limit_bytes=KERNEL_VMEM),
        name="example_squares",
    )(tokens, deltas, precond)
    return out[:, : priv // L, 0]


def clipped_kernel(factors_ref, tokens_ref, delta_ref, out_ref, acc_ref):
    quad = pl.program_id(0)
    examples = delta_ref.shape[1] // L
    weighted = jnp.concatenate(
        [
            (
                factors_ref[quad, example]
                * delta_ref[quad, example * L : (example + 1) * L, :].astype(jnp.float32)
            ).astype(jnp.bfloat16)
            for example in range(examples)
        ],
        axis=0,
    )

    @pl.when(quad == 0)
    def _():
        acc_ref[...] = jnp.zeros_like(acc_ref)

    for side in range(tokens_ref.shape[1]):
        acc_ref[side] += jnp.dot(
            tokens_ref[0, side], weighted, preferred_element_type=jnp.float32
        )

    @pl.when(quad == pl.num_programs(0) - 1)
    def _():
        out_ref[...] = acc_ref[...].astype(out_ref.dtype)


def clipped_sum(factors, tokens, deltas):
    quads, sides, rows, _ = tokens.shape
    priv, cols = deltas.shape[1:]
    return pl.pallas_call(
        clipped_kernel,
        grid=(quads,),
        in_specs=[
            pl.BlockSpec(memory_space=pltpu.SMEM),
            pl.BlockSpec((1, sides, rows, priv), lambda q: (q, 0, 0, 0)),
            pl.BlockSpec(memory_space=pltpu.VMEM),
        ],
        out_specs=pl.BlockSpec((sides, rows, cols), lambda q: (0, 0, 0)),
        out_shape=jax.ShapeDtypeStruct((sides, rows, cols), jnp.bfloat16),
        scratch_shapes=[pltpu.VMEM((sides, rows, cols), jnp.float32)],
        compiler_params=pltpu.CompilerParams(vmem_limit_bytes=KERNEL_VMEM),
        name="clipped_sum",
    )(factors, tokens, deltas)


def on_device(
    public_tokens,
    public_targets,
    private_tokens,
    private_targets,
    token_counts,
    weight,
    public_moment,
    adam_first,
    adam_second,
    noise_draw,
):
    replicas = lax.axis_size("replica")
    along_x = [[x * SIDE + y for x in range(SIDE)] for y in range(SIDE)]
    along_y = [[x * SIDE + y for y in range(SIDE)] for x in range(SIDE)]
    same_class = [
        [r * SIDE * SIDE + x * SIDE + y for r in range(replicas) for y in range(SIDE)]
        for x in range(SIDE)
    ]
    quads = replicas // SIDE
    pub = public_tokens.shape[0]
    priv = private_tokens.shape[0]
    rows, cols = weight.shape
    examples_here = token_counts.shape[1]
    pub_rows = public_targets.shape[0]
    priv_rows = private_targets.shape[0]
    pub_all = quads * SIDE * pub_rows
    priv_all = quads * SIDE * priv_rows
    moves = to_class(replicas)

    local = live_block(token_counts, private_tokens.T, public_tokens.T)
    def across_x(sent):
        return lax.all_to_all(sent, "tile", 0, 0, tiled=True, axis_index_groups=along_x)

    targets = jnp.concatenate([public_targets, private_targets], axis=0)
    targets = targets.reshape(-1, replicas, cols).transpose(1, 0, 2)
    local = lax.ppermute(local, ("replica", "tile"), moves)
    targets = lax.all_to_all(targets, "replica", 0, 0, tiled=True)
    w_half = weight.astype(jnp.bfloat16)

    tokens = lax.all_gather(local, "replica", axis=0)
    tokens = tokens.reshape(quads, SIDE, rows, pub + priv)

    targets = targets.reshape(quads, 2, CORES, -1, cols).transpose(2, 1, 0, 3, 4)
    targets = across_x(targets.reshape(SIDE, -1, cols))
    w_group = across_x(everywhere(w_half, SIDE))
    targets = targets.reshape(SIDE, quads, pub_rows + priv_rows, cols).transpose(1, 0, 2, 3)
    targets = jnp.concatenate(
        [
            targets[:, :, :pub_rows].reshape(pub_all, cols),
            targets[:, :, pub_rows:].reshape(priv_all, cols),
        ],
        axis=0,
    )

    def by_owner(part, span):
        part = part.reshape(quads, SIDE, SIDE, span, cols)
        return part.transpose(2, 0, 1, 3, 4).reshape(SIDE, quads * SIDE * span, cols)

    def by_token(part, span):
        part = part.reshape(SIDE, quads, SIDE, span, cols)
        return part.transpose(1, 2, 0, 3, 4).reshape(quads, SIDE * SIDE * span, cols)

    out = jnp.einsum(
        "qxfn,xfk->qnk", tokens, w_group, preferred_element_type=jnp.float32
    ).astype(jnp.bfloat16)
    sent = jnp.concatenate(
        [by_owner(out[:, priv:], pub_rows), by_owner(out[:, :priv], priv_rows)], axis=1
    )
    got, (targets, tokens) = exchange(sent, "tile", along_y, (targets, tokens))
    total = jnp.sum(got.astype(jnp.float32), axis=0)
    delta = (total - targets.astype(jnp.float32)).astype(jnp.bfloat16)
    deltas, (tokens, public_moment) = exchange(
        everywhere(delta, SIDE), "tile", along_y, (tokens, public_moment)
    )
    public_delta = by_token(deltas[:, :pub_all], pub_rows)
    private_delta = by_token(deltas[:, pub_all:], priv_rows)

    def over_classes(part):
        got, _ = exchange(part.astype(jnp.bfloat16), "tile", along_x)
        return jnp.sum(got.astype(jnp.float32), axis=0)

    public_grad = over_classes(
        jnp.einsum(
            "qxfn,qnk->xfk",
            tokens[:, :, :, priv:],
            public_delta,
            preferred_element_type=jnp.float32,
        )
    ) / math.sqrt(pub * replicas)
    new_public = beta_public * public_moment + (1.0 - beta_public) * public_grad * public_grad
    precond = 1.0 / (jnp.sqrt(new_public) + public_epsilon)
    precond_group, _ = exchange(
        everywhere(precond.astype(jnp.bfloat16), SIDE), "tile", along_x
    )

    squares = example_squares(tokens, private_delta, precond_group)
    peers = replicas * SIDE
    squares, _ = exchange(everywhere(squares, peers), ("replica", "tile"), same_class)
    squares = jnp.sum(squares, axis=0)
    clip_norm = clip_factor * math.sqrt(L * D * Q)
    factors = clip_norm / jnp.maximum(jnp.sqrt(squares), clip_norm)
    summed = precond * over_classes(clipped_sum(factors, tokens, private_delta))

    examples_total = examples_here * replicas
    noise_scale = noise_level * clip_factor * math.sqrt(L)
    gradient = (summed + noise_scale * noise_draw) / examples_total
    new_first = beta_first * adam_first + (1.0 - beta_first) * gradient
    new_second = beta_second * adam_second + (1.0 - beta_second) * gradient * gradient
    first_hat = new_first / (1.0 - beta_first**2)
    second_hat = new_second / (1.0 - beta_second**2)
    new_weight = weight - learn_rate * first_hat / (jnp.sqrt(second_hat) + adam_epsilon)
    return (new_weight, new_first, new_second, new_public)


def solution(mesh):
    placed = (
        P("replica", "tile"),
        P(("replica", "tile"), None),
        P("replica", "tile"),
        P(("replica", "tile"), None),
        P("replica", None),
        P("tile", "replica"),
        P("tile", "replica"),
        P("tile", "replica"),
        P("tile", "replica"),
        P("tile", "replica"),
    )
    return jax.shard_map(
        on_device,
        mesh=mesh,
        in_specs=placed,
        out_specs=(
            P("tile", "replica"),
            P("tile", "replica"),
            P("tile", "replica"),
            P("tile", "replica"),
        ),
        check_vma=False,
    )
```

```python
import math

import jax
import jax.numpy as jnp
from jax import lax
from jax.experimental import pallas as pl
from jax.experimental.pallas import tpu as pltpu
from jax.sharding import PartitionSpec as P

D = 5120
L = 128
Q = 4096
CORES = 2
SIDE = 4
KERNEL_VMEM = 58 * 2**20


beta_first = 0.9
beta_second = 0.99
beta_public = 0.9
public_epsilon = 0.001
adam_epsilon = 1e-08
clip_factor = 0.6
noise_level = 4.0
learn_rate = 0.01


def exchange(sent, axis, groups, kept=()):
    sent, kept = lax.optimization_barrier((sent, kept))
    got = lax.all_to_all(sent, axis, 0, 0, tiled=True, axis_index_groups=groups)
    return lax.optimization_barrier((got, kept))


def everywhere(values, parts):
    return jnp.broadcast_to(values[None], (parts, *values.shape))


def to_class(replicas):
    tiles = SIDE * SIDE
    moves = []
    for replica in range(replicas):
        quad, inner = divmod(replica, CORES * 2)
        odd, core = divmod(inner, CORES)
        for tile in range(tiles):
            x, y = divmod(tile, SIDE)
            chip, side = x % 2, x // 2
            target = (quad * SIDE + chip * CORES + side) * tiles
            target = target + (odd + 2 * core) * SIDE + y
            moves.append((replica * tiles + tile, target))
    return moves


def live_kernel(counts_ref, private_ref, public_ref, out_ref):
    rows, priv = private_ref.shape
    slot = lax.broadcasted_iota(jnp.int32, (rows, L), 1)
    for example in range(priv // L):
        lanes = slice(example * L, (example + 1) * L)
        block = private_ref[:, lanes].astype(jnp.float32)
        block = jnp.where(slot < counts_ref[0, example], block, 0.0)
        out_ref[:, lanes] = block.astype(out_ref.dtype)
    out_ref[:, priv:] = public_ref[...]


def live_block(counts, private, public):
    return pl.pallas_call(
        live_kernel,
        in_specs=[
            pl.BlockSpec(memory_space=pltpu.SMEM),
            pl.BlockSpec(memory_space=pltpu.VMEM),
            pl.BlockSpec(memory_space=pltpu.VMEM),
        ],
        out_specs=pl.BlockSpec(memory_space=pltpu.VMEM),
        out_shape=jax.ShapeDtypeStruct(
            (private.shape[0], private.shape[1] + public.shape[1]), private.dtype
        ),
        name="live_block",
    )(counts, private, public)


def norms_kernel(tokens_ref, delta_ref, precond_ref, out_ref, wide_ref):
    sides, rows = tokens_ref.shape[1], tokens_ref.shape[2]
    quad = pl.program_id(0)

    @pl.when(quad == 0)
    def _():
        wide_ref[...] = precond_ref[...].astype(jnp.float32)

    examples = delta_ref.shape[1] // L
    row_at = lax.broadcasted_iota(jnp.int32, out_ref.shape[1:], 0)
    found = jnp.zeros(out_ref.shape[1:], jnp.float32)
    for example in range(examples):
        block_d = delta_ref[quad, example * L : (example + 1) * L, :]
        first = example * L
        acc = jnp.zeros((8, block_d.shape[1]), jnp.float32)
        for side in range(sides):
            grads = jnp.dot(
                tokens_ref[0, side, :, first : first + L],
                block_d,
                preferred_element_type=jnp.float32,
            )
            scaled = grads * wide_ref[side]
            acc = acc + jnp.sum((scaled * scaled).reshape(rows // 8, 8, -1), axis=0)
        found = jnp.where(row_at == example, jnp.sum(acc), found)
    out_ref[0] = found


def example_squares(tokens, deltas, precond):
    quads, sides, rows, _ = tokens.shape
    priv, cols = deltas.shape[1:]
    out = pl.pallas_call(
        norms_kernel,
        grid=(quads,),
        in_specs=[
            pl.BlockSpec((1, sides, rows, priv), lambda q: (q, 0, 0, 0)),
            pl.BlockSpec(memory_space=pltpu.VMEM),
            pl.BlockSpec(memory_space=pltpu.VMEM),
        ],
        out_specs=pl.BlockSpec((1, 8, L), lambda q: (q, 0, 0)),
        out_shape=jax.ShapeDtypeStruct((quads, 8, L), jnp.float32),
        scratch_shapes=[pltpu.VMEM(precond.shape, jnp.float32)],
        compiler_params=pltpu.CompilerParams(vmem_limit_bytes=KERNEL_VMEM),
        name="example_squares",
    )(tokens, deltas, precond)
    return out[:, : priv // L, 0]


def clipped_kernel(factors_ref, tokens_ref, delta_ref, out_ref, acc_ref):
    quad = pl.program_id(0)
    examples = delta_ref.shape[1] // L
    weighted = jnp.concatenate(
        [
            (
                factors_ref[quad, example]
                * delta_ref[quad, example * L : (example + 1) * L, :].astype(jnp.float32)
            ).astype(jnp.bfloat16)
            for example in range(examples)
        ],
        axis=0,
    )

    @pl.when(quad == 0)
    def _():
        acc_ref[...] = jnp.zeros_like(acc_ref)

    for side in range(tokens_ref.shape[1]):
        acc_ref[side] += jnp.dot(
            tokens_ref[0, side], weighted, preferred_element_type=jnp.float32
        )

    @pl.when(quad == pl.num_programs(0) - 1)
    def _():
        out_ref[...] = acc_ref[...].astype(out_ref.dtype)


def clipped_sum(factors, tokens, deltas):
    quads, sides, rows, _ = tokens.shape
    priv, cols = deltas.shape[1:]
    return pl.pallas_call(
        clipped_kernel,
        grid=(quads,),
        in_specs=[
            pl.BlockSpec(memory_space=pltpu.SMEM),
            pl.BlockSpec((1, sides, rows, priv), lambda q: (q, 0, 0, 0)),
            pl.BlockSpec(memory_space=pltpu.VMEM),
        ],
        out_specs=pl.BlockSpec((sides, rows, cols), lambda q: (0, 0, 0)),
        out_shape=jax.ShapeDtypeStruct((sides, rows, cols), jnp.bfloat16),
        scratch_shapes=[pltpu.VMEM((sides, rows, cols), jnp.float32)],
        compiler_params=pltpu.CompilerParams(vmem_limit_bytes=KERNEL_VMEM),
        name="clipped_sum",
    )(factors, tokens, deltas)


def on_device(
    public_tokens,
    public_targets,
    private_tokens,
    private_targets,
    token_counts,
    weight,
    public_moment,
    adam_first,
    adam_second,
    noise_draw,
):
    replicas = lax.axis_size("replica")
    along_x = [[x * SIDE + y for x in range(SIDE)] for y in range(SIDE)]
    by_side = [[x * SIDE + y for x in (0, 2, 1, 3)] for y in range(SIDE)]
    along_y = [[x * SIDE + y for y in range(SIDE)] for x in range(SIDE)]
    same_class = [
        [r * SIDE * SIDE + x * SIDE + y for r in range(replicas) for y in range(SIDE)]
        for x in range(SIDE)
    ]
    quads = replicas // SIDE
    pub = public_tokens.shape[0]
    priv = private_tokens.shape[0]
    rows, cols = weight.shape
    examples_here = token_counts.shape[1]
    pub_rows = public_targets.shape[0]
    priv_rows = private_targets.shape[0]
    pub_all = quads * SIDE * pub_rows
    priv_all = quads * SIDE * priv_rows
    moves = to_class(replicas)

    local = live_block(token_counts, private_tokens.T, public_tokens.T)
    def across_x(sent):
        return lax.all_to_all(sent, "tile", 0, 0, tiled=True, axis_index_groups=along_x)

    targets = jnp.concatenate([public_targets, private_targets], axis=0)
    targets = targets.reshape(-1, replicas, cols).transpose(1, 0, 2)
    local = lax.ppermute(local, ("replica", "tile"), moves)
    targets = lax.all_to_all(targets, "replica", 0, 0, tiled=True)
    w_half = weight.astype(jnp.bfloat16)

    tokens = lax.all_gather(local, "replica", axis=0)
    tokens = tokens.reshape(quads, SIDE, rows, pub + priv)

    targets = targets.reshape(quads, 2, CORES, -1, cols).transpose(2, 1, 0, 3, 4)
    targets = across_x(targets.reshape(SIDE, -1, cols))
    w_group = lax.all_to_all(
        everywhere(w_half, SIDE), "tile", 0, 0, tiled=True, axis_index_groups=by_side
    )
    targets = targets.reshape(SIDE, quads, pub_rows + priv_rows, cols).transpose(1, 0, 2, 3)
    targets = jnp.concatenate(
        [
            targets[:, :, :pub_rows].reshape(pub_all, cols),
            targets[:, :, pub_rows:].reshape(priv_all, cols),
        ],
        axis=0,
    )

    def by_owner(part, span):
        part = part.reshape(quads, SIDE, SIDE, span, cols)
        return part.transpose(2, 0, 1, 3, 4).reshape(SIDE, quads * SIDE * span, cols)

    def by_token(part, span):
        part = part.reshape(SIDE, quads, SIDE, span, cols)
        return part.transpose(1, 2, 0, 3, 4).reshape(quads, SIDE * SIDE * span, cols)

    out = jnp.einsum(
        "qxfn,xfk->qnk", tokens, w_group, preferred_element_type=jnp.float32
    ).astype(jnp.bfloat16)
    sent = jnp.concatenate(
        [by_owner(out[:, priv:], pub_rows), by_owner(out[:, :priv], priv_rows)], axis=1
    )
    got, (targets, tokens) = exchange(sent, "tile", along_y, (targets, tokens))
    total = jnp.sum(got.astype(jnp.float32), axis=0)
    delta = (total - targets.astype(jnp.float32)).astype(jnp.bfloat16)
    deltas, (tokens, public_moment) = exchange(
        everywhere(delta, SIDE), "tile", along_y, (tokens, public_moment)
    )
    public_delta = by_token(deltas[:, :pub_all], pub_rows)
    private_delta = by_token(deltas[:, pub_all:], priv_rows)

    def over_classes(part):
        got, _ = exchange(part.astype(jnp.bfloat16), "tile", by_side)
        return jnp.sum(got.astype(jnp.float32), axis=0)

    public_grad = over_classes(
        jnp.einsum(
            "qxfn,qnk->xfk",
            tokens[:, :, :, priv:],
            public_delta,
            preferred_element_type=jnp.float32,
        )
    ) / math.sqrt(pub * replicas)
    new_public = beta_public * public_moment + (1.0 - beta_public) * public_grad * public_grad
    precond = 1.0 / (jnp.sqrt(new_public) + public_epsilon)
    precond_group, _ = exchange(
        everywhere(precond.astype(jnp.bfloat16), SIDE), "tile", by_side
    )

    squares = example_squares(tokens, private_delta, precond_group)
    peers = replicas * SIDE
    squares, _ = exchange(everywhere(squares, peers), ("replica", "tile"), same_class)
    squares = jnp.sum(squares, axis=0)
    clip_norm = clip_factor * math.sqrt(L * D * Q)
    factors = clip_norm / jnp.maximum(jnp.sqrt(squares), clip_norm)
    summed = precond * over_classes(clipped_sum(factors, tokens, private_delta))

    examples_total = examples_here * replicas
    noise_scale = noise_level * clip_factor * math.sqrt(L)
    gradient = (summed + noise_scale * noise_draw) / examples_total
    new_first = beta_first * adam_first + (1.0 - beta_first) * gradient
    new_second = beta_second * adam_second + (1.0 - beta_second) * gradient * gradient
    first_hat = new_first / (1.0 - beta_first**2)
    second_hat = new_second / (1.0 - beta_second**2)
    new_weight = weight - learn_rate * first_hat / (jnp.sqrt(second_hat) + adam_epsilon)
    return (new_weight, new_first, new_second, new_public)


def solution(mesh):
    placed = (
        P("replica", "tile"),
        P(("replica", "tile"), None),
        P("replica", "tile"),
        P(("replica", "tile"), None),
        P("replica", None),
        P("tile", "replica"),
        P("tile", "replica"),
        P("tile", "replica"),
        P("tile", "replica"),
        P("tile", "replica"),
    )
    return jax.shard_map(
        on_device,
        mesh=mesh,
        in_specs=placed,
        out_specs=(
            P("tile", "replica"),
            P("tile", "replica"),
            P("tile", "replica"),
            P("tile", "replica"),
        ),
        check_vma=False,
    )
```

```python
import math

import jax
import jax.numpy as jnp
from jax import lax
from jax.experimental import pallas as pl
from jax.experimental.pallas import tpu as pltpu
from jax.sharding import PartitionSpec as P

D = 5120
L = 128
Q = 4096
CORES = 2
SIDE = 4
KERNEL_VMEM = 52 * 2**20


beta_first = 0.9
beta_second = 0.99
beta_public = 0.9
public_epsilon = 0.001
adam_epsilon = 1e-08
clip_factor = 0.6
noise_level = 4.0
learn_rate = 0.01


def exchange(sent, axis, groups, kept=()):
    sent, kept = lax.optimization_barrier((sent, kept))
    got = lax.all_to_all(sent, axis, 0, 0, tiled=True, axis_index_groups=groups)
    return lax.optimization_barrier((got, kept))


def everywhere(values, parts):
    return jnp.broadcast_to(values[None], (parts, *values.shape))


def to_class(replicas):
    tiles = SIDE * SIDE
    moves = []
    for replica in range(replicas):
        quad, inner = divmod(replica, CORES * 2)
        odd, core = divmod(inner, CORES)
        for tile in range(tiles):
            x, y = divmod(tile, SIDE)
            chip, side = x % 2, x // 2
            target = (quad * SIDE + chip * CORES + side) * tiles
            target = target + (odd + 2 * core) * SIDE + y
            moves.append((replica * tiles + tile, target))
    return moves


def live_kernel(counts_ref, private_ref, public_ref, out_ref):
    rows, priv = private_ref.shape
    slot = lax.broadcasted_iota(jnp.int32, (rows, L), 1)
    for example in range(priv // L):
        lanes = slice(example * L, (example + 1) * L)
        block = private_ref[:, lanes].astype(jnp.float32)
        block = jnp.where(slot < counts_ref[0, example], block, 0.0)
        out_ref[:, lanes] = block.astype(out_ref.dtype)
    out_ref[:, priv:] = public_ref[...]


def live_block(counts, private, public):
    return pl.pallas_call(
        live_kernel,
        in_specs=[
            pl.BlockSpec(memory_space=pltpu.SMEM),
            pl.BlockSpec(memory_space=pltpu.VMEM),
            pl.BlockSpec(memory_space=pltpu.VMEM),
        ],
        out_specs=pl.BlockSpec(memory_space=pltpu.VMEM),
        out_shape=jax.ShapeDtypeStruct(
            (private.shape[0], private.shape[1] + public.shape[1]), private.dtype
        ),
        name="live_block",
    )(counts, private, public)


def norms_kernel(tokens_ref, delta_ref, precond_ref, out_ref, wide_ref):
    sides, rows = tokens_ref.shape[1], tokens_ref.shape[2]
    quad = pl.program_id(0)

    @pl.when(quad == 0)
    def _():
        wide_ref[...] = precond_ref[...].astype(jnp.float32)

    examples = delta_ref.shape[1] // L
    row_at = lax.broadcasted_iota(jnp.int32, out_ref.shape[1:], 0)
    found = jnp.zeros(out_ref.shape[1:], jnp.float32)
    for example in range(examples):
        block_d = delta_ref[quad, example * L : (example + 1) * L, :]
        first = example * L
        acc = jnp.zeros((8, block_d.shape[1]), jnp.float32)
        for side in range(sides):
            grads = jnp.dot(
                tokens_ref[0, side, :, first : first + L],
                block_d,
                preferred_element_type=jnp.float32,
            )
            scaled = grads * wide_ref[side]
            acc = acc + jnp.sum((scaled * scaled).reshape(rows // 8, 8, -1), axis=0)
        found = jnp.where(row_at == example, jnp.sum(acc), found)
    out_ref[0] = found


def example_squares(tokens, deltas, precond):
    quads, sides, rows, _ = tokens.shape
    priv, cols = deltas.shape[1:]
    out = pl.pallas_call(
        norms_kernel,
        grid=(quads,),
        in_specs=[
            pl.BlockSpec((1, sides, rows, priv), lambda q: (q, 0, 0, 0)),
            pl.BlockSpec(memory_space=pltpu.VMEM),
            pl.BlockSpec(memory_space=pltpu.VMEM),
        ],
        out_specs=pl.BlockSpec((1, 8, L), lambda q: (q, 0, 0)),
        out_shape=jax.ShapeDtypeStruct((quads, 8, L), jnp.float32),
        scratch_shapes=[pltpu.VMEM(precond.shape, jnp.float32)],
        compiler_params=pltpu.CompilerParams(vmem_limit_bytes=KERNEL_VMEM),
        name="example_squares",
    )(tokens, deltas, precond)
    return out[:, : priv // L, 0]


def clipped_kernel(factors_ref, tokens_ref, delta_ref, out_ref, acc_ref):
    quad = pl.program_id(0)
    examples = delta_ref.shape[1] // L
    weighted = jnp.concatenate(
        [
            (
                factors_ref[quad, example]
                * delta_ref[quad, example * L : (example + 1) * L, :].astype(jnp.float32)
            ).astype(jnp.bfloat16)
            for example in range(examples)
        ],
        axis=0,
    )

    @pl.when(quad == 0)
    def _():
        acc_ref[...] = jnp.zeros_like(acc_ref)

    for side in range(tokens_ref.shape[1]):
        acc_ref[side] += jnp.dot(
            tokens_ref[0, side], weighted, preferred_element_type=jnp.float32
        )

    @pl.when(quad == pl.num_programs(0) - 1)
    def _():
        out_ref[...] = acc_ref[...].astype(out_ref.dtype)


def clipped_sum(factors, tokens, deltas):
    quads, sides, rows, _ = tokens.shape
    priv, cols = deltas.shape[1:]
    return pl.pallas_call(
        clipped_kernel,
        grid=(quads,),
        in_specs=[
            pl.BlockSpec(memory_space=pltpu.SMEM),
            pl.BlockSpec((1, sides, rows, priv), lambda q: (q, 0, 0, 0)),
            pl.BlockSpec(memory_space=pltpu.VMEM),
        ],
        out_specs=pl.BlockSpec((sides, rows, cols), lambda q: (0, 0, 0)),
        out_shape=jax.ShapeDtypeStruct((sides, rows, cols), jnp.bfloat16),
        scratch_shapes=[pltpu.VMEM((sides, rows, cols), jnp.float32)],
        compiler_params=pltpu.CompilerParams(vmem_limit_bytes=KERNEL_VMEM),
        name="clipped_sum",
    )(factors, tokens, deltas)


def on_device(
    public_tokens,
    public_targets,
    private_tokens,
    private_targets,
    token_counts,
    weight,
    public_moment,
    adam_first,
    adam_second,
    noise_draw,
):
    replicas = lax.axis_size("replica")
    along_x = [[x * SIDE + y for x in range(SIDE)] for y in range(SIDE)]
    by_side = [[x * SIDE + y for x in (0, 2, 1, 3)] for y in range(SIDE)]
    along_y = [[x * SIDE + y for y in range(SIDE)] for x in range(SIDE)]
    same_class = [
        [r * SIDE * SIDE + x * SIDE + y for r in range(replicas) for y in range(SIDE)]
        for x in range(SIDE)
    ]
    quads = replicas // SIDE
    pub = public_tokens.shape[0]
    priv = private_tokens.shape[0]
    rows, cols = weight.shape
    examples_here = token_counts.shape[1]
    pub_rows = public_targets.shape[0]
    priv_rows = private_targets.shape[0]
    pub_all = quads * SIDE * pub_rows
    priv_all = quads * SIDE * priv_rows
    moves = to_class(replicas)

    local = live_block(token_counts, private_tokens.T, public_tokens.T)
    def across_x(sent):
        return lax.all_to_all(sent, "tile", 0, 0, tiled=True, axis_index_groups=along_x)

    targets = jnp.concatenate([public_targets, private_targets], axis=0)
    targets = targets.reshape(-1, replicas, cols).transpose(1, 0, 2)
    local = lax.ppermute(local, ("replica", "tile"), moves)
    targets = lax.all_to_all(targets, "replica", 0, 0, tiled=True)
    w_half = weight.astype(jnp.bfloat16)

    tokens = lax.all_gather(local, "replica", axis=0)
    tokens = tokens.reshape(quads, SIDE, rows, pub + priv)

    targets = targets.reshape(quads, 2, CORES, -1, cols).transpose(2, 1, 0, 3, 4)
    targets = across_x(targets.reshape(SIDE, -1, cols))
    w_group = lax.all_to_all(
        everywhere(w_half, SIDE), "tile", 0, 0, tiled=True, axis_index_groups=by_side
    )
    targets = targets.reshape(SIDE, quads, pub_rows + priv_rows, cols).transpose(1, 0, 2, 3)
    targets = jnp.concatenate(
        [
            targets[:, :, :pub_rows].reshape(pub_all, cols),
            targets[:, :, pub_rows:].reshape(priv_all, cols),
        ],
        axis=0,
    )

    def by_owner(part, span):
        part = part.reshape(quads, SIDE, SIDE, span, cols)
        return part.transpose(2, 0, 1, 3, 4).reshape(SIDE, quads * SIDE * span, cols)

    def by_token(part, span):
        part = part.reshape(SIDE, quads, SIDE, span, cols)
        return part.transpose(1, 2, 0, 3, 4).reshape(quads, SIDE * SIDE * span, cols)

    out = jnp.einsum(
        "qxfn,xfk->qnk", tokens, w_group, preferred_element_type=jnp.float32
    ).astype(jnp.bfloat16)
    sent = jnp.concatenate(
        [by_owner(out[:, priv:], pub_rows), by_owner(out[:, :priv], priv_rows)], axis=1
    )
    got, (targets, tokens) = exchange(sent, "tile", along_y, (targets, tokens))
    total = jnp.sum(got.astype(jnp.float32), axis=0)
    delta = (total - targets.astype(jnp.float32)).astype(jnp.bfloat16)
    deltas, (tokens, public_moment) = exchange(
        everywhere(delta, SIDE), "tile", along_y, (tokens, public_moment)
    )
    public_delta = by_token(deltas[:, :pub_all], pub_rows)
    private_delta = by_token(deltas[:, pub_all:], priv_rows)

    def over_classes(part):
        got, _ = exchange(part.astype(jnp.bfloat16), "tile", by_side)
        return jnp.sum(got.astype(jnp.float32), axis=0)

    public_grad = over_classes(
        jnp.einsum(
            "qxfn,qnk->xfk",
            tokens[:, :, :, priv:],
            public_delta,
            preferred_element_type=jnp.float32,
        )
    ) / math.sqrt(pub * replicas)
    new_public = beta_public * public_moment + (1.0 - beta_public) * public_grad * public_grad
    precond = 1.0 / (jnp.sqrt(new_public) + public_epsilon)
    precond_group, _ = exchange(
        everywhere(precond.astype(jnp.bfloat16), SIDE), "tile", by_side
    )

    squares = example_squares(tokens, private_delta, precond_group)
    peers = replicas * SIDE
    squares, _ = exchange(everywhere(squares, peers), ("replica", "tile"), same_class)
    squares = jnp.sum(squares, axis=0)
    clip_norm = clip_factor * math.sqrt(L * D * Q)
    factors = clip_norm / jnp.maximum(jnp.sqrt(squares), clip_norm)
    summed = precond * over_classes(clipped_sum(factors, tokens, private_delta))

    examples_total = examples_here * replicas
    noise_scale = noise_level * clip_factor * math.sqrt(L)
    gradient = (summed + noise_scale * noise_draw) / examples_total
    new_first = beta_first * adam_first + (1.0 - beta_first) * gradient
    new_second = beta_second * adam_second + (1.0 - beta_second) * gradient * gradient
    first_hat = new_first / (1.0 - beta_first**2)
    second_hat = new_second / (1.0 - beta_second**2)
    new_weight = weight - learn_rate * first_hat / (jnp.sqrt(second_hat) + adam_epsilon)
    return (new_weight, new_first, new_second, new_public)


def solution(mesh):
    placed = (
        P("replica", "tile"),
        P(("replica", "tile"), None),
        P("replica", "tile"),
        P(("replica", "tile"), None),
        P("replica", None),
        P("tile", "replica"),
        P("tile", "replica"),
        P("tile", "replica"),
        P("tile", "replica"),
        P("tile", "replica"),
    )
    return jax.shard_map(
        on_device,
        mesh=mesh,
        in_specs=placed,
        out_specs=(
            P("tile", "replica"),
            P("tile", "replica"),
            P("tile", "replica"),
            P("tile", "replica"),
        ),
        check_vma=False,
    )
```
